32 devices in a mesh: grp: 4 (over y, x), space: 8 (over z, core).
Axes of the slice: x: 2, y: 2, z: 4, core: 2. Of those that a mesh axis runs over, the one named last changes fastest.
Arguments:
- features: bfloat16 [4, 128, 128, 128], P('grp', 'space'), may hold values from -6 to 6
- weights: bfloat16 [27, 128, 128], replicated, may hold values from -0.109375 to 0.109375
- cotangent: bfloat16 [4, 128, 128, 128], P('grp', 'space'), may hold values from -6 to 6
- kernel_map: int32 [4, 128, 27], P('grp', 'space'), may hold values from -1 to 127, as said below
- counts: int32 [4, 8], P('grp', 'space'), may hold values from 4 to 16
Outputs:
- output: bfloat16 [4, 128, 128, 128], P('grp', 'space')
- input_grad: bfloat16 [4, 128, 128, 128], P('grp', 'space')
- weight_grad: float32 [3456, 128], P('space')
The draws below stay inside these ranges and needn't reach their ends.
Inputs may be any that keep to these rules, and one draw needn't show every extreme that they name: `kernel_map`: the centre offset k = 27 div 2 maps every block to itself. Otherwise an entry for an output block b on slab d = b div 16 is -1 or lies in [d * 16 - 4, (d + 1) * 16 + 4) within the sample. The live blocks of a device are its first counts slots.
All inputs are finite; a program needn't handle non-finite values.
Results may differ from the reference program's by a relative error of at most 0.005.
Values may be sent and summed in bfloat16 or wider, within the bound.
A program may use at most 64 MiB of HBM per device.

```python
import jax
import jax.numpy as jnp
from jax import lax

ROWS = 128
CIN = 128
COUT = 128
K = 27
H = 4
NB = 16
BLOCKS = 128
N_GRP = 4
N_SPACE = 8


def draw_kernel_map(key, part):
    block_ids = jnp.arange(BLOCKS, dtype=jnp.int32)
    slab = block_ids // NB
    lowest = jnp.maximum(slab * NB - H, 0)
    highest = jnp.minimum((slab + 1) * NB + H, BLOCKS)
    first_key, second_key = jax.random.split(jax.random.fold_in(key, 11))
    raw = jax.random.randint(first_key, (N_GRP, BLOCKS, K), 0, 1 << 20)
    source = lowest[None, :, None] + raw % (highest - lowest)[None, :, None]
    keep = jax.random.randint(second_key, (N_GRP, BLOCKS, K), 0, 10) < 7
    source = jnp.where(keep, source, -1)
    centre = jnp.arange(K, dtype=jnp.int32) == K // 2
    source = jnp.where(centre[None, None, :], block_ids[None, :, None], source)
    return source.astype(jnp.int32)


def plant(drawn, rng, low, high):
    longest = drawn.shape.index(max(drawn.shape))
    spots = []
    for shift in (0, 1):
        where = [jax.random.randint(jax.random.fold_in(rng, axis), (), 0, length) for axis, length in enumerate(drawn.shape)]
        where[longest] = (where[longest] + shift) % drawn.shape[longest]
        spots.append(tuple(where))
    return drawn.at[spots[0]].set(low).at[spots[1]].set(high)


def block_scale(key, shape, cuts, smallest, largest):
    def one(dim, parts):
        heights = jax.random.uniform(jax.random.fold_in(jax.random.fold_in(key, 6), dim), (parts,), jnp.float32, smallest / len(cuts), largest / len(cuts))
        return jnp.repeat(jnp.exp(heights), shape[dim] // parts).reshape((-1,) + (1,) * (len(shape) - dim - 1))

    level = one(*cuts[0])
    for cut in cuts[1:]:
        level = level * one(*cut)
    return level


def noise(rng, dims, width, limit, cuts=(), kind=jnp.bfloat16):
    result = width * jax.random.normal(rng, dims, jnp.float32)
    if cuts:
        result = result * block_scale(rng, dims, cuts, -0.22, 0.18)
    return jnp.clip(result, -limit, limit).astype(kind)


def setup_inputs(seed: int = 0) -> dict:
    splits = jax.random.split(jax.random.key(seed), 6)
    return {
        "features": noise(splits[0], (N_GRP, BLOCKS, ROWS, CIN), 1.0, 6.0, ((0, 4), (1, 8))),
        "weights": noise(splits[1], (K, CIN, COUT), (K * CIN) ** -0.5, 0.109375),
        "cotangent": noise(splits[2], (N_GRP, BLOCKS, ROWS, COUT), 1.0, 6.0, ((0, 4), (1, 8))),
        "kernel_map": draw_kernel_map(jax.random.fold_in(splits[5], 71), 0),
        "counts": plant(jax.random.randint(splits[4], (N_GRP, N_SPACE), NB // 4, NB + 1), jax.random.fold_in(splits[4], 1), NB // 4, NB).astype(jnp.int32),
    }


def reference(features, weights, cotangent, kernel_map, counts):
    block_ids = jnp.arange(BLOCKS, dtype=jnp.int32)
    outputs = []
    input_grads = []
    weight_grad = jnp.zeros((K, CIN, COUT), jnp.float32)
    for group in range(N_GRP):
        slab_counts = jnp.take(counts[group], block_ids // NB, axis=0)
        live_mask = ((block_ids % NB) < slab_counts).astype(jnp.bfloat16)[:, None, None]
        masked = features[group] * live_mask
        grad_out = cotangent[group] * live_mask
        block_map = kernel_map[group]
        present = (block_map >= 0).astype(jnp.bfloat16)
        source = jnp.maximum(block_map, 0).astype(jnp.int32)

        def step(offset, carry):
            total, grad_in, wgrad = carry
            column = lax.dynamic_index_in_dim(source, offset, 1, keepdims=False)
            present_k = lax.dynamic_index_in_dim(present, offset, 1, keepdims=False)[:, None, None]
            gathered = jnp.take(masked, column, axis=0) * present_k
            kernel = lax.dynamic_index_in_dim(weights, offset, 0, keepdims=False)
            total = total + jnp.einsum('brc,co->bro', gathered, kernel, preferred_element_type=jnp.float32)
            term = jnp.einsum('bro,co->brc', grad_out, kernel, preferred_element_type=jnp.float32)
            grad_in = grad_in.at[column].add(term * present_k.astype(jnp.float32))
            piece = jnp.einsum('brc,bro->co', gathered, grad_out, preferred_element_type=jnp.float32)
            wgrad = lax.dynamic_update_index_in_dim(wgrad, lax.dynamic_index_in_dim(wgrad, offset, 0, keepdims=False) + piece, offset, 0)
            return total, grad_in, wgrad

        start = (jnp.zeros((BLOCKS, ROWS, COUT), jnp.float32), jnp.zeros((BLOCKS, ROWS, CIN), jnp.float32), weight_grad)
        total, grad_in, weight_grad = lax.fori_loop(0, K, step, start)
        live_float = live_mask.astype(jnp.float32)
        outputs.append((total * live_float).astype(jnp.bfloat16))
        input_grads.append((grad_in * live_float).astype(jnp.bfloat16))
    return jnp.stack(outputs), jnp.stack(input_grads), weight_grad.reshape(K * CIN, COUT)
```

```python
import functools

import jax
import jax.numpy as jnp
from jax import lax
from jax.experimental import pallas as pl
from jax.experimental.pallas import tpu as pltpu
from jax.sharding import PartitionSpec as P

H = 4
WIDE = 2 * H
SPAN = 7
DEPTH = 4
BF16, F32 = jnp.bfloat16, jnp.float32
VMEM = pl.BlockSpec(memory_space=pltpu.VMEM)
FAR = pl.BlockSpec(memory_space=pl.ANY)
SMEM = pl.BlockSpec(memory_space=pltpu.SMEM)


def window_start(g, groups, unit, rows):
    return pl.multiple_of(g * unit - (g // (groups - 1)) * (groups * unit - rows), 16)


def main_kernel(
    groups, space, unit, rows, padded, piped,
    counts, block_map, feat, w_far, cot_far,
    out_far, ig_far, wg_far,
    w, cot, turned, blocks, ext, top, edge, fin, wg, tab, idx,
    flat, part, r0, p1, r1, p2, r2, r3,
    sl, so, sh, qh, sr, qr, s0, q0, s1, q1, s2, q2, s3, q3,
):
    g = lax.axis_index("grp")
    s = lax.axis_index("space")
    half = space // 2
    z, c = s // 2, s % 2
    slots, height, cin = feat.shape
    offsets = block_map.shape[1]
    near = slots + 2 * H
    empty = slots * offsets
    base = empty + 1
    live = counts[0, 0]
    partner = (g, z * 2 + (1 - c))
    grp_peers = [((g + d) % groups, s) for d in range(1, groups)]
    z_peers = [(g, ((z + d) % half) * 2 + c) for d in range(1, half)]
    copy = pltpu.make_async_copy

    load_top = copy(feat.at[pl.ds(slots - H, H)], top, sl.at[4])
    load_cot = copy(cot_far, cot, sl.at[0])
    load_w = copy(w_far, w.at[pl.ds(offsets, offsets)], sl.at[1])
    load_feat = copy(feat, ext.at[pl.ds(1 + H, slots)], sl.at[2])
    load_top.start()
    load_cot.start()
    load_w.start()
    load_feat.start()

    barrier = pltpu.get_barrier_semaphore()
    fixed = [partner] + grp_peers + z_peers
    for peer in fixed:
        pl.semaphore_signal(barrier, inc=1, device_id=peer, device_id_type=pl.DeviceIdType.MESH)
    across = s - 1 + 2 * c
    has_across = jnp.logical_and(across >= 0, across < space)

    @pl.when(has_across)
    def _():
        pl.semaphore_signal(barrier, inc=1, device_id=(g, across), device_id_type=pl.DeviceIdType.MESH)

    row = lax.broadcasted_iota(jnp.int32, (slots, offsets), 0)
    lane = lax.broadcasted_iota(jnp.int32, (1, offsets), 1)
    source = block_map[...]
    local = source - (s * slots - H)
    dead = jnp.logical_and(local - H >= live, local < slots + H)
    skip = jnp.logical_or(jnp.logical_or(source < 0, row >= live), dead)
    place = jnp.where(skip, -1, local)
    tab[...] = jnp.full(tab.shape, empty, jnp.int32)
    tab[0:slots, 0:offsets] = place + base

    def pick(mask):
        found = jnp.max(jnp.where(mask, row, -1), axis=0, keepdims=True)
        return jnp.where(found < 0, empty, found * offsets + lane)

    for a in range(near):
        at = slots + (slots + a if a < H else a - H if a < H + slots else a)
        tab[at : at + 1, 0:offsets] = pick(place == a)
    for b in range(slots):
        same = jnp.logical_and(place == place[b : b + 1, :], row < b)
        tab[slots + near + b : slots + near + b + 1, 0:offsets] = pick(same)
    load_idx = copy(tab, idx, sl.at[3])
    load_idx.start()

    zero = jnp.zeros((height, cin), BF16)
    blocks[empty] = zero
    ext[0] = zero
    edge[2 * H] = zero
    load_top.wait()
    for i in range(H):
        top[i] = top[i] * jnp.where(slots - H + i < live, 1.0, 0.0).astype(BF16)

    def remote(src, dst, send, recv, peer):
        return pltpu.make_async_remote_copy(
            src_ref=src, dst_ref=dst, send_sem=send, recv_sem=recv,
            device_id=peer, device_id_type=pl.DeviceIdType.MESH,
        )

    halo_down = remote(feat.at[pl.ds(0, H)], ext.at[pl.ds(1 + H + slots, H)], sh.at[0], qh.at[0], (g, s - 1))
    halo_up = remote(top, ext.at[pl.ds(1, H)], sh.at[1], qh.at[1], (g, s + 1))
    rim = 2 * slots
    down = remote(fin.at[pl.ds(rim, H)], edge.at[pl.ds(H, H)], sr.at[0], qr.at[0], (g, s - 1))
    up = remote(fin.at[pl.ds(rim + H, H)], edge.at[pl.ds(0, H)], sr.at[1], qr.at[1], (g, s + 1))
    has_down, has_up = s > 0, s < space - 1

    with jax.named_scope("barrier"):
        pl.semaphore_wait(barrier, len(fixed) + has_across.astype(jnp.int32))

    @pl.when(has_down)
    def _():
        halo_down.start()

    @pl.when(has_up)
    def _():
        halo_up.start()

    load_cot.wait()
    load_idx.wait()

    def turn_cot(b, carry):
        turned[b] = cot[b].T
        return carry

    def turn_ext(i, carry):
        blocks[base + i] = ext[1 + i].T
        return carry

    def flip(k, carry):
        w[k] = w[offsets + k].T
        return carry

    part_rows = cot.shape[2] // 2

    def build(b, carry):
        for top_row in range(0, cot.shape[2], part_rows):
            lines = pl.ds(top_row, part_rows)
            mine = turned[b, lines, :]

            def fetch(k):
                return mine + blocks[idx[slots + near + b, k], lines, :]

            ahead = [fetch(k) for k in range(DEPTH)]
            for k in range(offsets):
                if k + DEPTH < offsets:
                    ahead.append(fetch(k + DEPTH))
                blocks[b * offsets + k, lines, :] = ahead[k]
        return carry

    with jax.named_scope("turncot"):
        lax.fori_loop(0, slots, turn_cot, 0, unroll=8)
    load_feat.wait()
    with jax.named_scope("turn"):
        lax.fori_loop(H, H + slots, turn_ext, 0, unroll=8)
    load_w.wait()
    with jax.named_scope("flip"):
        lax.fori_loop(0, offsets, flip, 0, unroll=9 if offsets % 9 == 0 else 1)
    built = slots // 2
    with jax.named_scope("build"):
        lax.fori_loop(0, built, build, 0)

    @pl.when(has_down)
    def _():
        with jax.named_scope("halo1"):
            halo_up.wait_recv()

    @pl.when(jnp.logical_not(has_down))
    def _():
        for i in range(H):
            ext[1 + i] = zero

    @pl.when(has_up)
    def _():
        with jax.named_scope("halo2"):
            halo_down.wait_recv()

    @pl.when(jnp.logical_not(has_up))
    def _():
        for i in range(H):
            ext[1 + H + slots + i] = zero

    parts = slots // WIDE
    chunks = -(-offsets // SPAN)
    direct = rows == padded

    def nth(t):
        return jnp.where(t == 0, 0, jnp.where(t == 1, half - 1, t - 1)) if piped else t

    def weight_chunk(t):
        p = nth(t)
        back = jnp.where(t == 1, chunks * SPAN - offsets, 0) if piped else 0
        start = p * SPAN - back
        rhs = [
            jnp.concatenate([ext[idx[b, start + k] - empty] for b in range(slots)], axis=0)
            for k in range(SPAN)
        ]
        lhs = jnp.concatenate([turned[b] for b in range(slots)], axis=1)
        got = jnp.dot(lhs, jnp.concatenate(rhs, axis=1), preferred_element_type=F32)
        into = part if direct else flat
        for k in range(SPAN):
            to = start + k
            if piped:
                taken = jnp.logical_and(t == chunks - 1, to >= (chunks - 1) * SPAN - (chunks * SPAN - offsets))
                to = jnp.where(taken, offsets + to - (chunks - 1) * SPAN + 1, to)
            at = pl.multiple_of(to * cin, cin)
            into[pl.ds(at, cin), :] = got[:, k * cin : (k + 1) * cin].astype(BF16).T

    def gather_chunk(n):
        kind = jnp.where(n >= parts, offsets, 0)
        lhs = jnp.concatenate([w[kind + k] for k in range(offsets)], axis=1)
        rhs = [
            jnp.concatenate([blocks[idx[n * WIDE + j, k]] for j in range(WIDE)], axis=1)
            for k in range(offsets)
        ]
        got = jnp.dot(lhs, jnp.concatenate(rhs, axis=0), preferred_element_type=F32)
        own = jnp.logical_and(n >= parts, n < 2 * parts)
        for j in range(WIDE):
            i = jnp.where(own, n - parts, n) * WIDE + j
            below = jnp.logical_and(own, i < H)
            above = jnp.logical_and(own, i >= slots - H)
            extra = jnp.where(below, i, jnp.where(above, i - slots + 2 * H, 2 * H))
            factor = jnp.where(jnp.logical_or(n == 2 * parts, i < live), 1.0, 0.0).astype(F32)
            value = got[:, j * height : (j + 1) * height].T + edge[extra].astype(F32)
            fin[n * WIDE + j] = (value * factor).astype(BF16)

    def store(q, near_ref, far_ref, first, sem):
        return copy(near_ref.at[pl.ds(first + q * WIDE, WIDE)], far_ref.at[pl.ds(q * WIDE, WIDE)], sem)

    def piece(p):
        return pl.ds(pl.multiple_of(p * padded, 16), padded)

    here = window_start(g, groups, unit, padded)

    def copy0(i):
        return remote(part.at[piece(2 * i + 1 - c)], r0.at[i], s0.at[i], q0.at[i], partner)

    def copy1(i, d):
        there = window_start((g + d) % groups, groups, unit, padded)
        return remote(
            p1.at[i, pl.ds(there, unit)], r1.at[i, d - 1], s1.at[i, d - 1], q1.at[i, d - 1], grp_peers[d - 1]
        )

    def copy2(i, slot):
        return remote(p2.at[i], r2.at[slot], s2.at[i], q2.at[slot], (g, 2 * i + c))

    def copy3(d):
        return remote(r3.at[0], r3.at[d], s3.at[d - 1], q3.at[d - 1], grp_peers[d - 1])

    def event0(t):
        i = nth(t)
        copy0(i).start()

    def event1(t):
        i = nth(t)
        with jax.named_scope("w0"):
            copy0(i).wait_recv()
        p1[i] = (part[piece(2 * i + c), :].astype(F32) + r0[i].astype(F32)).astype(BF16)
        for d in range(1, groups):
            copy1(i, d).start()

    def event2(t):
        i = nth(t)
        total = p1[i, pl.ds(here, unit), :].astype(F32)
        with jax.named_scope("w1"):
            for d in range(1, groups):
                copy1(i, d).wait_recv()
        for d in range(1, groups):
            total = total + r1[i, d - 1].astype(F32)
        p2[i] = total.astype(BF16)

        @pl.when(z != i)
        def _():
            copy2(i, z).start()

    def event3():
        r2[z] = p2[z]

        def arrive(i, carry):
            @pl.when(z != i)
            def _():
                copy2(i, i).wait_recv()

            return carry

        with jax.named_scope("w2"):
            lax.fori_loop(0, half, arrive, 0)
        total = jnp.zeros((unit, wg.shape[1]), F32)
        for i in range(half):
            total = total + r2[i].astype(F32)
        r3[0] = total.astype(BF16)
        for d in range(1, groups):
            copy3(d).start()

    def span_of(event, first, past):
        lax.fori_loop(first, past, lambda i, carry: (event(i), carry)[1], 0)

    def each(step, lag, event):
        if piped:
            i = step - lag

            @pl.when(jnp.logical_and(i >= 0, i < half))
            def _():
                event(i)

        else:

            @pl.when(step == chunks - 1 + lag)
            def _():
                span_of(event, 0, half)

    steps = chunks + 3 + 2 * parts

    def body(step, carry):
        work = step - chunks - 2

        @pl.when(step < chunks)
        def _():
            with jax.named_scope("wg"):
                weight_chunk(step)

        if not direct:

            @pl.when(step == chunks - 1)
            def _():
                for p in range(space):
                    part[p * padded : p * padded + rows, :] = flat[p * rows : (p + 1) * rows, :]
                    part[p * padded + rows : (p + 1) * padded, :] = jnp.zeros((padded - rows, part.shape[1]), BF16)

        each(step, 0, event0)

        @pl.when(step == chunks)
        def _():
            with jax.named_scope("turn2"):
                lax.fori_loop(0, H, turn_ext, 0, unroll=H)
                lax.fori_loop(H + slots, near, turn_ext, 0, unroll=H)

        @pl.when(step == chunks + 1)
        def _():
            with jax.named_scope("build"):
                lax.fori_loop(built, slots, build, 0)

        @pl.when(work >= 0)
        def _():
            n = jnp.where(work == 0, 2 * parts, work - 1)

            @pl.when(n == parts)
            def _():
                @pl.when(has_down)
                def _():
                    up.wait_recv()

                @pl.when(jnp.logical_not(has_down))
                def _():
                    for i in range(H):
                        edge[i] = zero

                @pl.when(has_up)
                def _():
                    down.wait_recv()

                @pl.when(jnp.logical_not(has_up))
                def _():
                    for i in range(H):
                        edge[H + i] = zero

            with jax.named_scope("gather"):
                gather_chunk(n)

            @pl.when(n < parts)
            def _():
                store(n, fin, out_far, 0, so.at[n]).start()

            @pl.when(jnp.logical_and(n >= parts, n < 2 * parts))
            def _():
                store(n - parts, fin, ig_far, slots, so.at[n]).start()

            @pl.when(n == 2 * parts)
            def _():
                @pl.when(has_down)
                def _():
                    down.start()

                @pl.when(has_up)
                def _():
                    up.start()

        each(step, 1, event1)
        if piped:
            first = step - chunks - 1

            @pl.when(jnp.logical_and(first >= 0, first < half - 1))
            def _():
                span_of(event2, first, jnp.where(first == half - 2, half, first + 1))

        else:

            @pl.when(step == chunks + 2)
            def _():
                span_of(event2, 0, half)

        @pl.when(step == steps - 1 - parts)
        def _():
            event3()

        return carry

    lax.fori_loop(0, steps, body, 0)

    with jax.named_scope("w3"):
        for d in range(1, groups):
            copy3(d).wait_recv()
    for j in range(groups):
        at = min(j * unit, padded - unit)
        wg[at : at + unit, :] = r3[(g - j + groups) % groups].astype(F32)
    store_wg = copy(wg.at[pl.ds(0, rows)], wg_far, so.at[2 * parts])
    store_wg.start()

    with jax.named_scope("drain"):

        @pl.when(has_down)
        def _():
            halo_down.wait_send()
            down.wait_send()

        @pl.when(has_up)
        def _():
            halo_up.wait_send()
            up.wait_send()

        def drain(i, carry):
            copy0(i).wait_send()
            for d in range(1, groups):
                copy1(i, d).wait_send()

            @pl.when(z != i)
            def _():
                copy2(i, z).wait_send()

            return carry

        lax.fori_loop(0, half, drain, 0)
        for d in range(1, groups):
            copy3(d).wait_send()

        def stored(q, carry):
            store(q, fin, out_far, 0, so.at[q]).wait()
            store(q, fin, ig_far, slots, so.at[parts + q]).wait()
            return carry

        lax.fori_loop(0, parts, stored, 0)
        store_wg.wait()


def finish_kernel(out_in, ig_in, wg_in, out_far, ig_far, wg_far, store):
    stores = [
        pltpu.make_async_copy(a, b, store.at[i])
        for i, (a, b) in enumerate([(out_in, out_far), (ig_in, ig_far), (wg_in, wg_far)])
    ]
    for item in stores:
        item.start()
    for item in stores:
        item.wait()


def per_device(features, weights, cotangent, kernel_map, counts):
    voxels = features[0]
    slots, height, cin = voxels.shape
    offsets, _, cout = weights.shape
    space = lax.axis_size("space")
    groups = lax.axis_size("grp")
    near = slots + 2 * H

    half = space // 2
    deep = offsets * cin
    rows = deep // space
    padded = -(-rows // 16) * 16
    unit = -(-padded // (16 * groups)) * 16
    chunks = -(-offsets // SPAN)
    long = chunks * SPAN * cin
    direct = rows == padded
    piped = direct and half == chunks and 2 * rows <= SPAN * cin
    dma = pltpu.SemaphoreType.DMA
    vmem = pltpu.VMEM
    table = 2 * slots + near
    shapes = [((slots, height, cout), BF16), ((slots, height, cin), BF16), ((rows, cout), F32)]

    def stay(x):
        return pltpu.with_memory_space_constraint(x, pltpu.HBM)

    results = pl.pallas_call(
        functools.partial(main_kernel, groups, space, unit, rows, padded, piped),
        out_shape=tuple(vmem(*x) for x in shapes),
        in_specs=[SMEM, VMEM] + [FAR] * 3,
        out_specs=(FAR,) * 3,
        scratch_shapes=[
            vmem((2 * offsets, cin, cout), BF16),
            vmem((slots, height, cout), BF16),
            vmem((slots, cout, height), BF16),
            vmem((slots * offsets + 1 + near, cin, height), BF16),
            vmem((near + 1, height, cin), BF16),
            vmem((H, height, cin), BF16),
            vmem((2 * H + 1, height, cin), BF16),
            vmem((2 * slots + 2 * H, height, cin), BF16),
            vmem((padded, cout), F32),
            vmem((table, 128), jnp.int32),
            pltpu.SMEM((table, 128), jnp.int32),
            vmem((16 if direct else long, cout), BF16),
            vmem((max(long, deep) if direct else space * padded, cout), BF16),
            vmem((half, padded, cout), BF16),
            vmem((half, padded, cout), BF16),
            vmem((half, groups - 1, unit, cout), BF16),
            vmem((half, unit, cout), BF16),
            vmem((half, unit, cout), BF16),
            vmem((groups, unit, cout), BF16),
            dma((5,)),
            dma((2 * (slots // WIDE) + 1,)),
            dma((2,)), dma((2,)),
            dma((2,)), dma((2,)),
            dma((half,)), dma((half,)),
            dma((half, groups - 1)), dma((half, groups - 1)),
            dma((half,)), dma((half,)),
            dma((groups - 1,)), dma((groups - 1,)),
        ],
        compiler_params=pltpu.CompilerParams(
            collective_id=0, has_side_effects=True, vmem_limit_bytes=48 * 1024 * 1024
        ),
        name="main",
    )(counts, kernel_map[0], stay(voxels), stay(weights), stay(cotangent[0]))
    output, input_grad, wg = pl.pallas_call(
        finish_kernel,
        out_shape=tuple(jax.ShapeDtypeStruct(*x) for x in shapes),
        in_specs=[FAR] * 3,
        out_specs=(FAR,) * 3,
        scratch_shapes=[dma((3,))],
        compiler_params=pltpu.CompilerParams(vmem_limit_bytes=4 * 1024 * 1024),
        name="finish",
    )(*results)
    return output[None], input_grad[None], wg


def solution(mesh):
    in_specs = (
        P("grp", "space", None, None),
        P(),
        P("grp", "space", None, None),
        P("grp", "space", None),
        P("grp", "space"),
    )
    out_specs = (P("grp", "space", None, None), P("grp", "space", None, None), P("space", None))
    return jax.shard_map(
        per_device, mesh=mesh, in_specs=in_specs, out_specs=out_specs, check_vma=False
    )
```

```python
import functools

import jax
import jax.numpy as jnp
from jax import lax
from jax.experimental import pallas as pl
from jax.experimental.pallas import tpu as pltpu
from jax.sharding import PartitionSpec as P

H = 4
WIDE = 2 * H
SPAN = 7
DEPTH = 4
BF16, F32 = jnp.bfloat16, jnp.float32
VMEM = pl.BlockSpec(memory_space=pltpu.VMEM)
FAR = pl.BlockSpec(memory_space=pl.ANY)


def window_start(g, groups, unit, rows):
    return pl.multiple_of(g * unit - (g // (groups - 1)) * (groups * unit - rows), 16)


def main_kernel(
    groups, space, unit, rows, padded, piped,
    counts_far, map_far, feat, w_far, cot_far,
    out_far, ig_far, wg_far,
    w, cot, turned, blocks, ext, top, edge, fin, tab, idx, counts, block_map,
    flat, part, r0, p1, r1, p2, r2, r3,
    sl, sh, qh, sr, qr, s0, q0, s1, q1, s2, q2, s3, q3,
):
    g = lax.axis_index("grp")
    s = lax.axis_index("space")
    half = space // 2
    z, c = s // 2, s % 2
    slots, height, cin = feat.shape
    offsets = block_map.shape[1]
    near = slots + 2 * H
    empty = slots * offsets
    base = empty + 1
    partner = (g, z * 2 + (1 - c))
    grp_peers = [((g + d) % groups, s) for d in range(1, groups)]
    z_peers = [(g, ((z + d) % half) * 2 + c) for d in range(1, half)]
    copy = pltpu.make_async_copy

    load_counts = copy(counts_far, counts, sl.at[5])
    load_map = copy(map_far, block_map, sl.at[6])
    load_counts.start()
    load_map.start()
    load_top = copy(feat.at[pl.ds(slots - H, H)], top, sl.at[4])
    load_cot = copy(cot_far, cot, sl.at[0])
    load_w = copy(w_far, w.at[pl.ds(offsets, offsets)], sl.at[1])
    load_feat = copy(feat, ext.at[pl.ds(1 + H, slots)], sl.at[2])
    load_top.start()
    load_cot.start()
    load_feat.start()
    load_w.start()

    barrier = pltpu.get_barrier_semaphore()
    fixed = [partner] + grp_peers + z_peers
    for peer in fixed:
        pl.semaphore_signal(barrier, inc=1, device_id=peer, device_id_type=pl.DeviceIdType.MESH)
    across = s - 1 + 2 * c
    has_across = jnp.logical_and(across >= 0, across < space)

    @pl.when(has_across)
    def _():
        pl.semaphore_signal(barrier, inc=1, device_id=(g, across), device_id_type=pl.DeviceIdType.MESH)

    load_counts.wait()
    load_map.wait()
    live = counts[0, 0]

    row = lax.broadcasted_iota(jnp.int32, (slots, offsets), 0)
    lane = lax.broadcasted_iota(jnp.int32, (1, offsets), 1)
    source = block_map[...]
    local = source - (s * slots - H)
    dead = jnp.logical_and(local - H >= live, local < slots + H)
    skip = jnp.logical_or(jnp.logical_or(source < 0, row >= live), dead)
    place = jnp.where(skip, -1, local)
    tab[...] = jnp.full(tab.shape, empty, jnp.int32)
    tab[0:slots, 0:offsets] = place + base

    def pick(mask):
        found = jnp.max(jnp.where(mask, row, -1), axis=0, keepdims=True)
        return jnp.where(found < 0, empty, found * offsets + lane)

    def grad_row(a):
        if H <= a < 2 * H:
            return slots - 2 * H + a - H
        if slots <= a < slots + H:
            return slots - H + a - slots
        return slots + a if a < H else a - 2 * H if a < slots else a

    for a in range(near):
        at = slots + grad_row(a)
        tab[at : at + 1, 0:offsets] = pick(place == a)
    for b in range(slots):
        same = jnp.logical_and(place == place[b : b + 1, :], row < b)
        tab[slots + near + b : slots + near + b + 1, 0:offsets] = pick(same)
    load_idx = copy(tab, idx, sl.at[3])
    load_idx.start()

    zero = jnp.zeros((height, cin), BF16)
    blocks[empty] = zero
    ext[0] = zero
    edge[2 * H] = zero
    load_top.wait()
    for i in range(H):
        top[i] = top[i] * jnp.where(slots - H + i < live, 1.0, 0.0).astype(BF16)

    def remote(src, dst, send, recv, peer):
        return pltpu.make_async_remote_copy(
            src_ref=src, dst_ref=dst, send_sem=send, recv_sem=recv,
            device_id=peer, device_id_type=pl.DeviceIdType.MESH,
        )

    halo_down = remote(feat.at[pl.ds(0, H)], ext.at[pl.ds(1 + H + slots, H)], sh.at[0], qh.at[0], (g, s - 1))
    halo_up = remote(top, ext.at[pl.ds(1, H)], sh.at[1], qh.at[1], (g, s + 1))
    rim = 2 * slots
    down = remote(fin.at[pl.ds(rim, H)], edge.at[pl.ds(H, H)], sr.at[0], qr.at[0], (g, s - 1))
    up = remote(fin.at[pl.ds(rim + H, H)], edge.at[pl.ds(0, H)], sr.at[1], qr.at[1], (g, s + 1))
    has_down, has_up = s > 0, s < space - 1

    with jax.named_scope("barrier"):
        pl.semaphore_wait(barrier, len(fixed) + has_across.astype(jnp.int32))

    @pl.when(has_down)
    def _():
        halo_down.start()

    @pl.when(has_up)
    def _():
        halo_up.start()

    load_cot.wait()

    def turn_cot(b, carry):
        turned[b] = cot[b].T
        return carry

    def turn_ext(i, carry):
        blocks[base + i] = ext[1 + i].T
        return carry

    def flip(k, carry):
        w[k] = w[offsets + k].T
        return carry

    part_rows = cot.shape[2] // 2

    def build(b, carry):
        for top_row in range(0, cot.shape[2], part_rows):
            lines = pl.ds(top_row, part_rows)
            mine = turned[b, lines, :]

            def fetch(k):
                return mine + blocks[idx[slots + near + b, k], lines, :]

            ahead = [fetch(k) for k in range(DEPTH)]
            for k in range(offsets):
                if k + DEPTH < offsets:
                    ahead.append(fetch(k + DEPTH))
                blocks[b * offsets + k, lines, :] = ahead[k]
        return carry

    with jax.named_scope("turncot"):
        lax.fori_loop(0, slots, turn_cot, 0, unroll=8)
    load_feat.wait()
    with jax.named_scope("turn"):
        lax.fori_loop(H, H + slots, turn_ext, 0, unroll=8)
    load_w.wait()
    with jax.named_scope("flip"):
        lax.fori_loop(0, offsets, flip, 0, unroll=9 if offsets % 9 == 0 else 1)
    load_idx.wait()
    built = slots * 5 // 8
    with jax.named_scope("build"):
        lax.fori_loop(0, built, build, 0)

    @pl.when(has_down)
    def _():
        with jax.named_scope("halo1"):
            halo_up.wait_recv()

    @pl.when(jnp.logical_not(has_down))
    def _():
        for i in range(H):
            ext[1 + i] = zero

    @pl.when(has_up)
    def _():
        with jax.named_scope("halo2"):
            halo_down.wait_recv()

    @pl.when(jnp.logical_not(has_up))
    def _():
        for i in range(H):
            ext[1 + H + slots + i] = zero

    parts = slots // WIDE
    chunks = -(-offsets // SPAN)
    direct = rows == padded

    def weight_chunk(t):
        start = t * SPAN
        rhs = [
            jnp.concatenate([ext[idx[b, start + k] - empty] for b in range(slots)], axis=0)
            for k in range(SPAN)
        ]
        lhs = jnp.concatenate([turned[b] for b in range(slots)], axis=1)
        got = jnp.dot(lhs, jnp.concatenate(rhs, axis=1), preferred_element_type=F32)
        into = part if direct else flat
        for k in range(SPAN):
            at = pl.multiple_of((start + k) * cin, cin)
            into[pl.ds(at, cin), :] = got[:, k * cin : (k + 1) * cin].astype(BF16).T

    def gather_chunk(n):
        kind = jnp.where(n >= parts, offsets, 0)
        lhs = jnp.concatenate([w[kind + k] for k in range(offsets)], axis=1)
        rhs = [
            jnp.concatenate([blocks[idx[n * WIDE + j, k]] for j in range(WIDE)], axis=1)
            for k in range(offsets)
        ]
        got = jnp.dot(lhs, jnp.concatenate(rhs, axis=0), preferred_element_type=F32)
        outer = n == 2 * parts - 1
        for j in range(WIDE):
            i = jnp.where(n < parts, n, n - parts) * WIDE + j
            i = jnp.where(n < parts, i, jnp.where(outer, j if j < H else slots - WIDE + j, i + H))
            extra = jnp.where(outer, j, 2 * H)
            factor = jnp.where(jnp.logical_or(n == 2 * parts, i < live), 1.0, 0.0).astype(F32)
            value = got[:, j * height : (j + 1) * height].T + edge[extra].astype(F32)
            fin[n * WIDE + j] = (value * factor).astype(BF16)

    def store_out(q):
        return copy(fin.at[pl.ds(q * WIDE, WIDE)], out_far.at[pl.ds(q * WIDE, WIDE)], sl.at[q])

    def store_inner(q):
        return copy(fin.at[pl.ds(slots + q * WIDE, WIDE)], ig_far.at[pl.ds(H + q * WIDE, WIDE)], sl.at[parts + q])

    def store_outer(side):
        at = 2 * slots - WIDE + side * H
        return copy(fin.at[pl.ds(at, H)], ig_far.at[pl.ds(side * (slots - H), H)], sl.at[2 * parts - 1 + side])

    def piece(p):
        return pl.ds(pl.multiple_of(p * padded, 16), padded)

    here = window_start(g, groups, unit, padded)

    def copy0(i):
        return remote(part.at[piece(2 * i + 1 - c)], r0.at[i], s0, q0.at[i], partner)

    def copy1(i, d):
        there = window_start((g + d) % groups, groups, unit, padded)
        return remote(
            p1.at[i, pl.ds(there, unit)], r1.at[i, d - 1], s1, q1.at[i], grp_peers[d - 1]
        )

    def copy2(i, slot):
        return remote(p2.at[i], r2.at[slot], s2, q2, (g, 2 * i + c))

    def wait(like, sem):
        copy(like, like, sem).wait()

    def copy3(d):
        return remote(r3.at[0], r3.at[d], s3, q3, grp_peers[d - 1])

    def event0(i):
        copy0(i).start()

    def event1(i):
        with jax.named_scope("w0"):
            copy0(i).wait_recv()
        p1[i] = (part[piece(2 * i + c), :].astype(F32) + r0[i].astype(F32)).astype(BF16)
        for d in range(1, groups):
            copy1(i, d).start()

    def event2(i):
        total = p1[i, pl.ds(here, unit), :].astype(F32)
        with jax.named_scope("w1"):
            wait(r1.at[i], q1.at[i])
        for d in range(1, groups):
            total = total + r1[i, d - 1].astype(F32)
        p2[i] = total.astype(BF16)

        @pl.when(z != i)
        def _():
            copy2(i, z).start()

    def event3():
        with jax.named_scope("w2"):
            wait(r2.at[pl.ds(0, half - 1)], q2)
        r2[z] = p2[z]
        total = jnp.zeros((unit, cot.shape[2]), F32)
        for i in range(half):
            total = total + r2[i].astype(F32)
        r3[0] = total.astype(BF16)
        for d in range(1, groups):
            copy3(d).start()

    def span_of(event, first, past):
        lax.fori_loop(first, past, lambda i, carry: (event(i), carry)[1], 0)

    def each(step, lag, event):
        if piped:
            i = step - lag

            @pl.when(jnp.logical_and(i >= 0, i < half))
            def _():
                event(i)

        else:

            @pl.when(step == chunks - 1 + lag)
            def _():
                span_of(event, 0, half)

    steps = chunks + 3 + 2 * parts

    def body(step, carry):
        work = step - chunks - 2

        @pl.when(step < chunks)
        def _():
            with jax.named_scope("wg"):
                weight_chunk(step)

        if not direct:

            @pl.when(step == chunks - 1)
            def _():
                for p in range(space):
                    part[p * padded : p * padded + rows, :] = flat[p * rows : (p + 1) * rows, :]
                    part[p * padded + rows : (p + 1) * padded, :] = jnp.zeros((padded - rows, part.shape[1]), BF16)

        each(step, 0, event0)

        @pl.when(step == chunks)
        def _():
            with jax.named_scope("turn2"):
                lax.fori_loop(0, H, turn_ext, 0, unroll=H)
                lax.fori_loop(H + slots, near, turn_ext, 0, unroll=H)

        @pl.when(step == chunks + 1)
        def _():
            with jax.named_scope("build"):
                lax.fori_loop(built, slots, build, 0)

        @pl.when(work >= 0)
        def _():
            n = jnp.where(work == 0, 2 * parts, work - 1)

            @pl.when(n == 2 * parts - 1)
            def _():
                @pl.when(has_down)
                def _():
                    up.wait_recv()

                @pl.when(jnp.logical_not(has_down))
                def _():
                    for i in range(H):
                        edge[i] = zero

                @pl.when(has_up)
                def _():
                    down.wait_recv()

                @pl.when(jnp.logical_not(has_up))
                def _():
                    for i in range(H):
                        edge[H + i] = zero

            with jax.named_scope("gather"):
                gather_chunk(n)

            @pl.when(n < parts)
            def _():
                store_out(n).start()

            @pl.when(jnp.logical_and(n >= parts, n < 2 * parts - 1))
            def _():
                store_inner(n - parts).start()

            @pl.when(n == 2 * parts - 1)
            def _():
                store_outer(0).start()
                store_outer(1).start()

        each(step, 1, event1)
        if piped:
            first = step - chunks - 1

            @pl.when(jnp.logical_and(first >= 0, first < half - 1))
            def _():
                span_of(event2, first, jnp.where(first == half - 2, half, first + 1))

        else:

            @pl.when(step == chunks + 2)
            def _():
                span_of(event2, 0, half)

        @pl.when(work == 0)
        def _():
            @pl.when(has_down)
            def _():
                down.start()

            @pl.when(has_up)
            def _():
                up.start()

        @pl.when(step == (steps - 3 + (z + 1) // 2 if piped else steps - 1))
        def _():
            event3()

        return carry

    lax.fori_loop(0, steps, body, 0)

    with jax.named_scope("w3"):
        wait(r3.at[pl.ds(1, groups - 1)], q3)
    for j in range(groups):
        at = min(j * unit, padded - unit)
        length = min(unit, rows - at)
        wg_far[at : at + length, :] = r3[(g - j + groups) % groups, 0:length, :].astype(F32)

    with jax.named_scope("drain"):

        @pl.when(has_down)
        def _():
            halo_down.wait_send()
            down.wait_send()

        @pl.when(has_up)
        def _():
            halo_up.wait_send()
            up.wait_send()

        wait(r0, s0)
        wait(r1, s1)
        wait(r2.at[pl.ds(0, half - 1)], s2)
        wait(r3.at[pl.ds(1, groups - 1)], s3)

        def stored(q, carry):
            store_out(q).wait()
            return carry

        def stored_inner(q, carry):
            store_inner(q).wait()
            return carry

        lax.fori_loop(0, parts, stored, 0)
        lax.fori_loop(0, parts - 1, stored_inner, 0)
        store_outer(0).wait()
        store_outer(1).wait()


def finish_kernel(out_in, ig_in, wg_in, out_far, ig_far, wg_far, store):
    stores = [
        pltpu.make_async_copy(a, b, store.at[i])
        for i, (a, b) in enumerate([(out_in, out_far), (ig_in, ig_far), (wg_in, wg_far)])
    ]
    for item in stores:
        item.start()
    for item in stores:
        item.wait()


def per_device(features, weights, cotangent, kernel_map, counts):
    voxels = features[0]
    slots, height, cin = voxels.shape
    offsets, _, cout = weights.shape
    space = lax.axis_size("space")
    groups = lax.axis_size("grp")
    near = slots + 2 * H

    half = space // 2
    deep = offsets * cin
    rows = deep // space
    padded = -(-rows // 16) * 16
    unit = -(-padded // (16 * groups)) * 16
    chunks = -(-offsets // SPAN)
    long = chunks * SPAN * cin
    direct = rows == padded
    piped = direct and half == chunks and 2 * rows <= SPAN * cin
    dma = pltpu.SemaphoreType.DMA
    vmem = pltpu.VMEM
    table = 2 * slots + near
    shapes = [((slots, height, cout), BF16), ((slots, height, cin), BF16), ((rows, cout), F32)]

    def stay(x):
        return pltpu.with_memory_space_constraint(x, pltpu.HBM)

    results = pl.pallas_call(
        functools.partial(main_kernel, groups, space, unit, rows, padded, piped),
        out_shape=tuple(vmem(*x) for x in shapes),
        in_specs=[FAR] * 5,
        out_specs=(FAR, FAR, VMEM),
        scratch_shapes=[
            vmem((2 * offsets, cin, cout), BF16),
            vmem((slots, height, cout), BF16),
            vmem((slots, cout, height), BF16),
            vmem((slots * offsets + 1 + near, cin, height), BF16),
            vmem((near + 1, height, cin), BF16),
            vmem((H, height, cin), BF16),
            vmem((2 * H + 1, height, cin), BF16),
            vmem((2 * slots + 2 * H, height, cin), BF16),
            vmem((table, 128), jnp.int32),
            pltpu.SMEM((table, 128), jnp.int32),
            pltpu.SMEM((1, 1), jnp.int32),
            vmem((slots, offsets), jnp.int32),
            vmem((16 if direct else long, cout), BF16),
            vmem((max(long, deep) if direct else space * padded, cout), BF16),
            vmem((half, padded, cout), BF16),
            vmem((half, padded, cout), BF16),
            vmem((half, groups - 1, unit, cout), BF16),
            vmem((half, unit, cout), BF16),
            vmem((half, unit, cout), BF16),
            vmem((groups, unit, cout), BF16),
            dma((max(7, 2 * (slots // WIDE) + 2),)),
            dma((2,)), dma((2,)),
            dma((2,)), dma((2,)),
            dma, dma((half,)),
            dma, dma((half,)),
            dma, dma,
            dma, dma,
        ],
        compiler_params=pltpu.CompilerParams(
            collective_id=0, has_side_effects=True, vmem_limit_bytes=48 * 1024 * 1024
        ),
        name="main",
    )(counts, stay(kernel_map[0]), stay(voxels), stay(weights), stay(cotangent[0]))
    output, input_grad, wg = pl.pallas_call(
        finish_kernel,
        out_shape=tuple(jax.ShapeDtypeStruct(*x) for x in shapes),
        in_specs=[FAR] * 3,
        out_specs=(FAR,) * 3,
        scratch_shapes=[dma((3,))],
        compiler_params=pltpu.CompilerParams(vmem_limit_bytes=4 * 1024 * 1024),
        name="finish",
    )(*results)
    return output[None], input_grad[None], wg


def solution(mesh):
    in_specs = (
        P("grp", "space", None, None),
        P(),
        P("grp", "space", None, None),
        P("grp", "space", None),
        P("grp", "space"),
    )
    out_specs = (P("grp", "space", None, None), P("grp", "space", None, None), P("space", None))
    return jax.shard_map(
        per_device, mesh=mesh, in_specs=in_specs, out_specs=out_specs, check_vma=False
    )
```

```python
import functools

import jax
import jax.numpy as jnp
from jax import lax
from jax.experimental import pallas as pl
from jax.experimental.pallas import tpu as pltpu
from jax.sharding import PartitionSpec as P

H = 4
WIDE = 2 * H
SPAN = 7
BUILT, PAUSED = 11, 13
BF16, F32 = jnp.bfloat16, jnp.float32
VMEM = pl.BlockSpec(memory_space=pltpu.VMEM)
FAR = pl.BlockSpec(memory_space=pl.ANY)


def window_start(g, groups, unit, rows):
    return pl.multiple_of(g * unit - (g // (groups - 1)) * (groups * unit - rows), 16)


def main_kernel(
    groups, space, unit, rows, padded, piped,
    counts_far, map_far, feat, w_far, cot_far,
    fin, wg_far,
    w, cot, turned, blocks, ext, top, edge, tab, idx, counts, block_map,
    flat, part, r0, p1, r1, p2, r2, r3,
    sl, sh, qh, sr, qr, s0, q0, s1, q1, s2, q2, s3, q3,
):
    g = lax.axis_index("grp")
    s = lax.axis_index("space")
    half = space // 2
    z, c = s // 2, s % 2
    slots, height, cin = feat.shape
    offsets = block_map.shape[1]
    near = slots + 2 * H
    empty = slots * offsets
    base = empty + 1
    partner = (g, z * 2 + (1 - c))
    grp_peers = [((g + d) % groups, s) for d in range(1, groups)]
    z_peers = [(g, ((z + d) % half) * 2 + c) for d in range(1, half)]
    copy = pltpu.make_async_copy
    far = 3 - 2 * (g % 2)
    turns = [far, 2, 4 - far] if groups == 4 else list(range(1, groups))

    barrier = pltpu.get_barrier_semaphore()
    fixed = [partner] + grp_peers + z_peers
    for peer in fixed:
        pl.semaphore_signal(barrier, inc=1, device_id=peer, device_id_type=pl.DeviceIdType.MESH)
    across = s - 1 + 2 * c
    has_across = jnp.logical_and(across >= 0, across < space)

    @pl.when(has_across)
    def _():
        pl.semaphore_signal(barrier, inc=1, device_id=(g, across), device_id_type=pl.DeviceIdType.MESH)

    load_counts = copy(counts_far, counts, sl.at[5])
    load_map = copy(map_far, block_map, sl.at[6])
    load_counts.start()
    load_map.start()
    load_top = copy(feat.at[pl.ds(slots - H, H)], top, sl.at[4])
    load_cot = copy(cot_far, cot, sl.at[0])
    load_w = copy(w_far, w.at[pl.ds(offsets, offsets)], sl.at[1])
    load_feat = copy(feat, ext.at[pl.ds(1 + H, slots)], sl.at[2])
    load_top.start()
    load_cot.start()
    load_feat.start()
    load_w.start()

    zero = jnp.zeros((height, cin), BF16)
    blocks[empty] = zero
    ext[0] = zero
    edge[2 * H] = zero
    def remote(src, dst, send, recv, peer):
        return pltpu.make_async_remote_copy(
            src_ref=src, dst_ref=dst, send_sem=send, recv_sem=recv,
            device_id=peer, device_id_type=pl.DeviceIdType.MESH,
        )

    halo_down = remote(feat.at[pl.ds(0, H)], ext.at[pl.ds(1 + H + slots, H)], sh.at[0], qh.at[0], (g, s - 1))
    halo_up = remote(top, ext.at[pl.ds(1, H)], sh.at[1], qh.at[1], (g, s + 1))
    rim = 2 * slots
    down = remote(fin.at[pl.ds(rim, H)], edge.at[pl.ds(H, H)], sr.at[0], qr.at[0], (g, s - 1))
    up = remote(fin.at[pl.ds(rim + H, H)], edge.at[pl.ds(0, H)], sr.at[1], qr.at[1], (g, s + 1))
    has_down, has_up = s > 0, s < space - 1

    with jax.named_scope("barrier"):
        pl.semaphore_wait(barrier, len(fixed) + has_across.astype(jnp.int32))

    @pl.when(has_down)
    def _():
        halo_down.start()

    load_counts.wait()
    live = counts[0, 0]
    load_top.wait()
    for i in range(H):
        top[i] = top[i] * jnp.where(slots - H + i < live, 1.0, 0.0).astype(BF16)

    @pl.when(has_up)
    def _():
        halo_up.start()

    load_map.wait()

    row = lax.broadcasted_iota(jnp.int32, (slots, offsets), 0)
    lane = lax.broadcasted_iota(jnp.int32, (1, offsets), 1)
    source = block_map[...]
    local = source - (s * slots - H)
    dead = jnp.logical_and(local - H >= live, local < slots + H)
    skip = jnp.logical_or(jnp.logical_or(source < 0, row >= live), dead)
    place = jnp.where(skip, -1, local)
    tab[...] = jnp.full(tab.shape, empty, jnp.int32)
    tab[0:slots, 0:offsets] = place + base

    def pick(mask):
        found = jnp.max(jnp.where(mask, row, -1), axis=0, keepdims=True)
        return jnp.where(found < 0, empty, found * offsets + lane)

    def grad_row(a):
        if H <= a < 2 * H:
            return slots - 2 * H + a - H
        if slots <= a < slots + H:
            return slots - H + a - slots
        return slots + a if a < H else a - 2 * H if a < slots else a

    for a in range(near):
        at = slots + grad_row(a)
        tab[at : at + 1, 0:offsets] = pick(place == a)
    for b in range(slots):
        same = jnp.logical_and(place == place[b : b + 1, :], row < b)
        tab[slots + near + b : slots + near + b + 1, 0:offsets] = pick(same)
    load_idx = copy(tab, idx, sl.at[3])
    load_idx.start()

    load_cot.wait()

    def turn_cot(b, carry):
        turned[b] = cot[b].T
        return carry

    def turn_ext(i, carry):
        blocks[base + i] = ext[1 + i].T
        return carry

    def flip(k, carry):
        w[k] = w[offsets + k].T
        return carry

    def build(b, carry):
        mine = turned[b]

        def fetch(k):
            return mine + blocks[idx[slots + near + b, k]]

        ahead = fetch(0)
        for k in range(offsets):
            following = fetch(k + 1) if k + 1 < offsets else None
            blocks[b * offsets + k] = ahead
            ahead = following
        return carry

    with jax.named_scope("turncot"):
        lax.fori_loop(0, slots, turn_cot, 0, unroll=8)
    load_feat.wait()
    with jax.named_scope("turn"):
        lax.fori_loop(H, H + slots, turn_ext, 0, unroll=8)
    load_w.wait()
    with jax.named_scope("flip"):
        lax.fori_loop(0, offsets, flip, 0, unroll=9 if offsets % 9 == 0 else 1)
    load_idx.wait()
    built, paused = slots * BUILT // 16, slots * PAUSED // 16
    with jax.named_scope("build"):
        lax.fori_loop(0, built, build, 0)

    @pl.when(has_down)
    def _():
        with jax.named_scope("halo1"):
            halo_up.wait_recv()

    @pl.when(jnp.logical_not(has_down))
    def _():
        for i in range(H):
            ext[1 + i] = zero

    @pl.when(has_up)
    def _():
        with jax.named_scope("halo2"):
            halo_down.wait_recv()

    @pl.when(jnp.logical_not(has_up))
    def _():
        for i in range(H):
            ext[1 + H + slots + i] = zero

    parts = slots // WIDE
    chunks = -(-offsets // SPAN)
    direct = rows == padded

    def nth(t):
        return jnp.where(t == 0, 0, jnp.where(t == 1, half - 1, t - 1)) if piped else t

    def weight_chunk(t):
        spare = chunks * SPAN - offsets
        start = nth(t) * SPAN - (jnp.where(t == 1, spare, 0) if piped else 0)
        rhs = [
            jnp.concatenate([ext[idx[b, start + k] - empty] for b in range(slots)], axis=0)
            for k in range(SPAN)
        ]
        lhs = jnp.concatenate([turned[b] for b in range(slots)], axis=1)
        got = jnp.dot(lhs, jnp.concatenate(rhs, axis=1), preferred_element_type=F32)
        into = part if direct else flat
        for k in range(SPAN):
            to = start + k
            if piped and k >= SPAN - spare:
                to = jnp.where(t == chunks - 1, (chunks - 1) * SPAN + k, to)
            at = pl.multiple_of(to * cin, cin)
            into[pl.ds(at, cin), :] = got[:, k * cin : (k + 1) * cin].astype(BF16).T

    def gather_chunk(n):
        kind = jnp.where(n >= parts, offsets, 0)
        lhs = jnp.concatenate([w[kind + k] for k in range(offsets)], axis=1)
        rhs = [
            jnp.concatenate([blocks[idx[n * WIDE + j, k]] for j in range(WIDE)], axis=1)
            for k in range(offsets)
        ]
        got = jnp.dot(lhs, jnp.concatenate(rhs, axis=0), preferred_element_type=F32)
        outer = n == 2 * parts - 1
        for j in range(WIDE):
            i = jnp.where(n < parts, n, n - parts) * WIDE + j
            i = jnp.where(n < parts, i, jnp.where(outer, j if j < H else slots - WIDE + j, i + H))
            extra = jnp.where(outer, j, 2 * H)
            factor = jnp.where(jnp.logical_or(n == 2 * parts, i < live), 1.0, 0.0).astype(F32)
            value = got[:, j * height : (j + 1) * height].T + edge[extra].astype(F32)
            fin[n * WIDE + j] = (value * factor).astype(BF16)

    def piece(p):
        return pl.ds(pl.multiple_of(p * padded, 16), padded)

    here = window_start(g, groups, unit, padded)

    def copy0(i):
        return remote(part.at[piece(2 * i + 1 - c)], r0.at[i], s0, q0.at[i], partner)

    def copy1(i, d):
        there = window_start((g + d) % groups, groups, unit, padded)
        return remote(
            p1.at[i, pl.ds(there, unit)], r1.at[i, d - 1], s1, q1.at[i], ((g + d) % groups, s)
        )

    def copy2(i, slot):
        return remote(p2.at[i], r2.at[slot], s2, q2, (g, 2 * i + c))

    def wait(like, sem):
        copy(like, like, sem).wait()

    def copy3(d):
        return remote(r3.at[0], r3.at[d], s3, q3, ((g + d) % groups, s))

    def event0(t):
        i = nth(t)
        copy0(i).start()

    def event1(t):
        i = nth(t)
        with jax.named_scope("w0"):
            copy0(i).wait_recv()
        p1[i] = (part[piece(2 * i + c), :].astype(F32) + r0[i].astype(F32)).astype(BF16)
        for d in turns:
            copy1(i, d).start()

    def event2(t):
        i = nth(t)
        total = p1[i, pl.ds(here, unit), :].astype(F32)
        with jax.named_scope("w1"):
            wait(r1.at[i], q1.at[i])
        for d in range(1, groups):
            total = total + r1[i, d - 1].astype(F32)
        p2[i] = total.astype(BF16)

        @pl.when(z != i)
        def _():
            copy2(i, z).start()

    def event3():
        with jax.named_scope("w2"):
            wait(r2.at[pl.ds(0, half - 1)], q2)
        r2[z] = p2[z]
        total = jnp.zeros((unit, cot.shape[2]), F32)
        for i in range(half):
            total = total + r2[i].astype(F32)
        r3[0] = total.astype(BF16)
        for d in turns:
            copy3(d).start()

    def span_of(event, first, past):
        lax.fori_loop(first, past, lambda i, carry: (event(i), carry)[1], 0)

    def each(step, lag, event):
        if piped:
            i = step - lag

            @pl.when(jnp.logical_and(i >= 0, i < half))
            def _():
                event(i)

        else:

            @pl.when(step == chunks - 1 + lag)
            def _():
                span_of(event, 0, half)

    steps = chunks + 3 + 2 * parts

    def body(step, carry):
        work = step - chunks - 2

        @pl.when(step < chunks)
        def _():
            with jax.named_scope("wg"):
                weight_chunk(step)

        if not direct:

            @pl.when(step == chunks - 1)
            def _():
                for p in range(space):
                    part[p * padded : p * padded + rows, :] = flat[p * rows : (p + 1) * rows, :]
                    part[p * padded + rows : (p + 1) * padded, :] = jnp.zeros((padded - rows, part.shape[1]), BF16)

        each(step, 0, event0)

        @pl.when(step == chunks)
        def _():
            with jax.named_scope("turn2"):
                lax.fori_loop(0, H, turn_ext, 0, unroll=H)
                lax.fori_loop(H + slots, near, turn_ext, 0, unroll=H)

        @pl.when(jnp.logical_and(step >= chunks, work < 0))
        def _():
            with jax.named_scope("build"):
                first = jnp.where(step == chunks, built, paused)
                lax.fori_loop(first, jnp.where(step == chunks, paused, slots), build, 0)

        @pl.when(work >= 0)
        def _():
            n = jnp.where(work == 0, 2 * parts, work - 1)

            @pl.when(n == 2 * parts - 1)
            def _():
                @pl.when(has_down)
                def _():
                    up.wait_recv()

                @pl.when(jnp.logical_not(has_down))
                def _():
                    for i in range(H):
                        edge[i] = zero

                @pl.when(has_up)
                def _():
                    down.wait_recv()

                @pl.when(jnp.logical_not(has_up))
                def _():
                    for i in range(H):
                        edge[H + i] = zero

            with jax.named_scope("gather"):
                gather_chunk(n)

        each(step, 1, event1)
        if piped:
            first = step - chunks - 1

            @pl.when(jnp.logical_and(first >= 0, first < half - 1))
            def _():
                span_of(event2, first, jnp.where(first == half - 2, half, first + 1))

        else:

            @pl.when(step == chunks + 2)
            def _():
                span_of(event2, 0, half)

        @pl.when(work == 0)
        def _():
            @pl.when(has_down)
            def _():
                down.start()

            @pl.when(has_up)
            def _():
                up.start()

        @pl.when(step == (steps - 4 + 2 * jnp.minimum(z, 1) if piped else steps - 1))
        def _():
            event3()

        return carry

    lax.fori_loop(0, steps, body, 0)

    with jax.named_scope("w3"):
        wait(r3.at[pl.ds(1, groups - 1)], q3)
    for j in range(groups):
        at = min(j * unit, padded - unit)
        length = min(unit, rows - at)
        wg_far[at : at + length, :] = r3[(g - j + groups) % groups, 0:length, :].astype(F32)

    with jax.named_scope("drain"):

        @pl.when(has_down)
        def _():
            halo_down.wait_send()
            down.wait_send()

        @pl.when(has_up)
        def _():
            halo_up.wait_send()
            up.wait_send()

        wait(r0, s0)
        wait(r1, s1)
        wait(r2.at[pl.ds(0, half - 1)], s2)
        wait(r3.at[pl.ds(1, groups - 1)], s3)


def finish_kernel(fin, wg_in, out_far, ig_far, wg_far, store):
    slots = out_far.shape[0]
    inner = slots - 2 * H
    moves = [
        (fin.at[pl.ds(0, slots)], out_far),
        (fin.at[pl.ds(slots, inner)], ig_far.at[pl.ds(H, inner)]),
        (fin.at[pl.ds(slots + inner, H)], ig_far.at[pl.ds(0, H)]),
        (fin.at[pl.ds(2 * slots - H, H)], ig_far.at[pl.ds(slots - H, H)]),
        (wg_in, wg_far),
    ]
    stores = [pltpu.make_async_copy(a, b, store.at[i]) for i, (a, b) in enumerate(moves)]
    for item in stores:
        item.start()
    for item in stores:
        item.wait()


def per_device(features, weights, cotangent, kernel_map, counts):
    voxels = features[0]
    slots, height, cin = voxels.shape
    offsets, _, cout = weights.shape
    space = lax.axis_size("space")
    groups = lax.axis_size("grp")
    near = slots + 2 * H

    half = space // 2
    deep = offsets * cin
    rows = deep // space
    padded = -(-rows // 16) * 16
    unit = -(-padded // (16 * groups)) * 16
    chunks = -(-offsets // SPAN)
    long = chunks * SPAN * cin
    direct = rows == padded
    piped = direct and half == chunks and 2 * rows <= SPAN * cin
    dma = pltpu.SemaphoreType.DMA
    vmem = pltpu.VMEM
    table = 2 * slots + near
    shapes = [((slots, height, cout), BF16), ((slots, height, cin), BF16), ((rows, cout), F32)]

    def stay(x):
        return pltpu.with_memory_space_constraint(x, pltpu.HBM)

    results = pl.pallas_call(
        functools.partial(main_kernel, groups, space, unit, rows, padded, piped),
        out_shape=(vmem((2 * slots + 2 * H, height, cout), BF16), vmem(*shapes[2])),
        in_specs=[FAR] * 5,
        out_specs=(VMEM, VMEM),
        scratch_shapes=[
            vmem((2 * offsets, cin, cout), BF16),
            vmem((slots, height, cout), BF16),
            vmem((slots, cout, height), BF16),
            vmem((slots * offsets + 1 + near, cin, height), BF16),
            vmem((near + 1, height, cin), BF16),
            vmem((H, height, cin), BF16),
            vmem((2 * H + 1, height, cin), BF16),
            vmem((table, 128), jnp.int32),
            pltpu.SMEM((table, 128), jnp.int32),
            pltpu.SMEM((1, 1), jnp.int32),
            vmem((slots, offsets), jnp.int32),
            vmem((16 if direct else long, cout), BF16),
            vmem((max(long, deep) if direct else space * padded, cout), BF16),
            vmem((half, padded, cout), BF16),
            vmem((half, padded, cout), BF16),
            vmem((half, groups - 1, unit, cout), BF16),
            vmem((half, unit, cout), BF16),
            vmem((half, unit, cout), BF16),
            vmem((groups, unit, cout), BF16),
            dma((7,)),
            dma((2,)), dma((2,)),
            dma((2,)), dma((2,)),
            dma, dma((half,)),
            dma, dma((half,)),
            dma, dma,
            dma, dma,
        ],
        compiler_params=pltpu.CompilerParams(
            collective_id=0, has_side_effects=True, vmem_limit_bytes=48 * 1024 * 1024
        ),
        name="main",
    )(counts, stay(kernel_map[0]), stay(voxels), stay(weights), stay(cotangent[0]))
    output, input_grad, wg = pl.pallas_call(
        finish_kernel,
        out_shape=tuple(jax.ShapeDtypeStruct(*x) for x in shapes),
        in_specs=[FAR] * 2,
        out_specs=(FAR,) * 3,
        scratch_shapes=[dma((5,))],
        compiler_params=pltpu.CompilerParams(vmem_limit_bytes=4 * 1024 * 1024),
        name="finish",
    )(*results)
    return output[None], input_grad[None], wg


def solution(mesh):
    in_specs = (
        P("grp", "space", None, None),
        P(),
        P("grp", "space", None, None),
        P("grp", "space", None),
        P("grp", "space"),
    )
    out_specs = (P("grp", "space", None, None), P("grp", "space", None, None), P("space", None))
    return jax.shard_map(
        per_device, mesh=mesh, in_specs=in_specs, out_specs=out_specs, check_vma=False
    )
```

```python
import functools

import jax
import jax.numpy as jnp
from jax import lax
from jax.experimental import pallas as pl
from jax.experimental.pallas import tpu as pltpu
from jax.sharding import PartitionSpec as P

H = 4
WIDE = 2 * H
SPAN = 7
BUILT, PAUSED = 11, 13
BF16, F32 = jnp.bfloat16, jnp.float32
VMEM = pl.BlockSpec(memory_space=pltpu.VMEM)
FAR = pl.BlockSpec(memory_space=pl.ANY)


def window_start(g, groups, unit, rows):
    return pl.multiple_of(g * unit - (g // (groups - 1)) * (groups * unit - rows), 16)


def main_kernel(
    groups, space, unit, rows, padded, piped,
    counts_far, map_far, feat, w_far, cot_far,
    fin, wg_far,
    w, cot, turned, blocks, ext, top, edge, tab, idx, counts, block_map,
    flat, part, r0, p1, r1, p2, r2, r3,
    sl, sh, qh, sr, qr, s0, q0, s1, q1, s2, q2, s3, q3,
):
    g = lax.axis_index("grp")
    s = lax.axis_index("space")
    half = space // 2
    z, c = s // 2, s % 2
    slots, height, cin = feat.shape
    offsets = block_map.shape[1]
    near = slots + 2 * H
    empty = slots * offsets
    base = empty + 1
    partner = (g, z * 2 + (1 - c))
    grp_peers = [((g + d) % groups, s) for d in range(1, groups)]
    z_peers = [(g, ((z + d) % half) * 2 + c) for d in range(1, half)]
    copy = pltpu.make_async_copy
    far = 3 - 2 * (g % 2)
    turns = [far, 2, 4 - far] if groups == 4 else list(range(1, groups))

    barrier = pltpu.get_barrier_semaphore()
    fixed = [partner] + grp_peers + z_peers
    for peer in fixed:
        pl.semaphore_signal(barrier, inc=1, device_id=peer, device_id_type=pl.DeviceIdType.MESH)
    across = s - 1 + 2 * c
    has_across = jnp.logical_and(across >= 0, across < space)

    @pl.when(has_across)
    def _():
        pl.semaphore_signal(barrier, inc=1, device_id=(g, across), device_id_type=pl.DeviceIdType.MESH)

    load_counts = copy(counts_far, counts, sl.at[5])
    load_map = copy(map_far, block_map, sl.at[6])
    load_counts.start()
    load_map.start()
    load_top = copy(feat.at[pl.ds(slots - H, H)], top, sl.at[4])
    load_cot = copy(cot_far, cot, sl.at[0])
    load_w = copy(w_far, w.at[pl.ds(offsets, offsets)], sl.at[1])
    load_feat = copy(feat, ext.at[pl.ds(1 + H, slots)], sl.at[2])
    load_top.start()
    load_cot.start()
    load_feat.start()
    load_w.start()

    zero = jnp.zeros((height, cin), BF16)
    blocks[empty] = zero
    ext[0] = zero
    edge[2 * H] = zero
    def remote(src, dst, send, recv, peer):
        return pltpu.make_async_remote_copy(
            src_ref=src, dst_ref=dst, send_sem=send, recv_sem=recv,
            device_id=peer, device_id_type=pl.DeviceIdType.MESH,
        )

    halo_down = remote(feat.at[pl.ds(0, H)], ext.at[pl.ds(1 + H + slots, H)], sh.at[0], qh.at[0], (g, s - 1))
    halo_up = remote(top, ext.at[pl.ds(1, H)], sh.at[1], qh.at[1], (g, s + 1))
    rim = 2 * slots
    down = remote(fin.at[pl.ds(rim, H)], edge.at[pl.ds(H, H)], sr.at[0], qr.at[0], (g, s - 1))
    up = remote(fin.at[pl.ds(rim + H, H)], edge.at[pl.ds(0, H)], sr.at[1], qr.at[1], (g, s + 1))
    has_down, has_up = s > 0, s < space - 1

    with jax.named_scope("barrier"):
        pl.semaphore_wait(barrier, len(fixed) + has_across.astype(jnp.int32))

    @pl.when(has_down)
    def _():
        halo_down.start()

    load_counts.wait()
    live = counts[0, 0]
    load_top.wait()
    for i in range(H):
        top[i] = top[i] * jnp.where(slots - H + i < live, 1.0, 0.0).astype(BF16)

    @pl.when(has_up)
    def _():
        halo_up.start()

    load_map.wait()

    row = lax.broadcasted_iota(jnp.int32, (slots, offsets), 0)
    lane = lax.broadcasted_iota(jnp.int32, (1, offsets), 1)
    source = block_map[...]
    local = source - (s * slots - H)
    dead = jnp.logical_and(local - H >= live, local < slots + H)
    skip = jnp.logical_or(jnp.logical_or(source < 0, row >= live), dead)
    place = jnp.where(skip, -1, local)
    tab[...] = jnp.full(tab.shape, empty, jnp.int32)
    tab[0:slots, 0:offsets] = place + base

    def pick(mask):
        found = jnp.max(jnp.where(mask, row, -1), axis=0, keepdims=True)
        return jnp.where(found < 0, empty, found * offsets + lane)

    def grad_row(a):
        if H <= a < 2 * H:
            return slots - 2 * H + a - H
        if slots <= a < slots + H:
            return slots - H + a - slots
        return slots + a if a < H else a - 2 * H if a < slots else a

    for a in range(near):
        at = slots + grad_row(a)
        tab[at : at + 1, 0:offsets] = pick(place == a)
    for b in range(slots):
        same = jnp.logical_and(place == place[b : b + 1, :], row < b)
        tab[slots + near + b : slots + near + b + 1, 0:offsets] = pick(same)
    load_idx = copy(tab, idx, sl.at[3])
    load_idx.start()

    load_cot.wait()

    def turn_cot(b, carry):
        turned[b] = cot[b].T
        return carry

    def turn_ext(i, carry):
        blocks[base + i] = ext[1 + i].T
        return carry

    def flip(k, carry):
        w[k] = w[offsets + k].T
        return carry

    def build(b, carry):
        mine = turned[b]

        def fetch(k):
            return mine + blocks[idx[slots + near + b, k]]

        ahead = fetch(0)
        for k in range(offsets):
            following = fetch(k + 1) if k + 1 < offsets else None
            blocks[b * offsets + k] = ahead
            ahead = following
        return carry

    with jax.named_scope("turncot"):
        lax.fori_loop(0, slots, turn_cot, 0, unroll=8)
    load_feat.wait()
    with jax.named_scope("turn"):
        lax.fori_loop(H, H + slots, turn_ext, 0, unroll=8)
    load_w.wait()
    with jax.named_scope("flip"):
        lax.fori_loop(0, offsets, flip, 0, unroll=9 if offsets % 9 == 0 else 1)
    load_idx.wait()
    built, paused = slots * BUILT // 16, slots * PAUSED // 16
    with jax.named_scope("build"):
        lax.fori_loop(0, built, build, 0)

    @pl.when(has_down)
    def _():
        with jax.named_scope("halo1"):
            halo_up.wait_recv()

    @pl.when(jnp.logical_not(has_down))
    def _():
        for i in range(H):
            ext[1 + i] = zero

    @pl.when(has_up)
    def _():
        with jax.named_scope("halo2"):
            halo_down.wait_recv()

    @pl.when(jnp.logical_not(has_up))
    def _():
        for i in range(H):
            ext[1 + H + slots + i] = zero

    parts = slots // WIDE
    chunks = -(-offsets // SPAN)
    direct = rows == padded

    def nth(t):
        return jnp.where(t == 0, 0, jnp.where(t == 1, half - 1, t - 1)) if piped else t

    def weight_chunk(t):
        spare = chunks * SPAN - offsets
        start = nth(t) * SPAN - (jnp.where(t == 1, spare, 0) if piped else 0)
        rhs = [
            jnp.concatenate([ext[idx[b, start + k] - empty] for b in range(slots)], axis=0)
            for k in range(SPAN)
        ]
        lhs = jnp.concatenate([turned[b] for b in range(slots)], axis=1)
        got = jnp.dot(lhs, jnp.concatenate(rhs, axis=1), preferred_element_type=F32)
        into = part if direct else flat
        for k in range(SPAN):
            to = start + k
            if piped and k >= SPAN - spare:
                to = jnp.where(t == chunks - 1, (chunks - 1) * SPAN + k, to)
            at = pl.multiple_of(to * cin, cin)
            into[pl.ds(at, cin), :] = got[:, k * cin : (k + 1) * cin].astype(BF16).T

    def gather_chunk(n):
        kind = jnp.where(n >= parts, offsets, 0)
        lhs = jnp.concatenate([w[kind + k] for k in range(offsets)], axis=1)
        rhs = [
            jnp.concatenate([blocks[idx[n * WIDE + j, k]] for j in range(WIDE)], axis=1)
            for k in range(offsets)
        ]
        got = jnp.dot(lhs, jnp.concatenate(rhs, axis=0), preferred_element_type=F32)
        outer = n == 2 * parts - 1
        for j in range(WIDE):
            i = jnp.where(n < parts, n, n - parts) * WIDE + j
            i = jnp.where(n < parts, i, jnp.where(outer, j if j < H else slots - WIDE + j, i + H))
            extra = jnp.where(outer, j, 2 * H)
            factor = jnp.where(jnp.logical_or(n == 2 * parts, i < live), 1.0, 0.0).astype(F32)
            value = got[:, j * height : (j + 1) * height].T + edge[extra].astype(F32)
            fin[n * WIDE + j] = (value * factor).astype(BF16)

    def piece(p):
        return pl.ds(pl.multiple_of(p * padded, 16), padded)

    here = window_start(g, groups, unit, padded)

    def copy0(i):
        return remote(part.at[piece(2 * i + 1 - c)], r0.at[i], s0, q0.at[i], partner)

    def copy1(i, d):
        there = window_start((g + d) % groups, groups, unit, padded)
        return remote(
            p1.at[i, pl.ds(there, unit)], r1.at[i, d - 1], s1, q1.at[i], ((g + d) % groups, s)
        )

    def copy2(i, slot):
        return remote(p2.at[i], r2.at[slot], s2, q2, (g, 2 * i + c))

    def wait(like, sem):
        copy(like, like, sem).wait()

    def copy3(d):
        return remote(r3.at[0], r3.at[d], s3, q3, ((g + d) % groups, s))

    def event0(t):
        i = nth(t)
        copy0(i).start()

    def event1(t):
        i = nth(t)
        with jax.named_scope("w0"):
            copy0(i).wait_recv()
        p1[i] = (part[piece(2 * i + c), :].astype(F32) + r0[i].astype(F32)).astype(BF16)
        for d in turns:
            copy1(i, d).start()

    def event2(t):
        i = nth(t)
        total = p1[i, pl.ds(here, unit), :].astype(F32)
        with jax.named_scope("w1"):
            wait(r1.at[i], q1.at[i])
        for d in range(1, groups):
            total = total + r1[i, d - 1].astype(F32)
        p2[i] = total.astype(BF16)

        @pl.when(z != i)
        def _():
            copy2(i, z).start()

    def event3():
        with jax.named_scope("w2"):
            wait(r2.at[pl.ds(0, half - 1)], q2)
        r2[z] = p2[z]
        total = jnp.zeros((unit, cot.shape[2]), F32)
        for i in range(half):
            total = total + r2[i].astype(F32)
        r3[0] = total.astype(BF16)
        for d in turns:
            copy3(d).start()

    def span_of(event, first, past):
        lax.fori_loop(first, past, lambda i, carry: (event(i), carry)[1], 0)

    def each(step, lag, event):
        if piped:
            i = step - lag

            @pl.when(jnp.logical_and(i >= 0, i < half))
            def _():
                event(i)

        else:

            @pl.when(step == chunks - 1 + lag)
            def _():
                span_of(event, 0, half)

    steps = chunks + 3 + 2 * parts

    early = jnp.where(jnp.logical_and(z == 0, g == 0), 1, 0)

    def ready(step):
        counts_at = [jnp.minimum(z, 1), 2, half - early]
        number = jnp.where(step > chunks, half, 0)
        for j, value in enumerate(counts_at):
            number = jnp.where(step == chunks + 1 + j, value, number)
        return number

    def body(step, carry):
        work = step - chunks - 2

        @pl.when(step < chunks)
        def _():
            with jax.named_scope("wg"):
                weight_chunk(step)

        if not direct:

            @pl.when(step == chunks - 1)
            def _():
                for p in range(space):
                    part[p * padded : p * padded + rows, :] = flat[p * rows : (p + 1) * rows, :]
                    part[p * padded + rows : (p + 1) * padded, :] = jnp.zeros((padded - rows, part.shape[1]), BF16)

        each(step, 0, event0)

        @pl.when(step == chunks)
        def _():
            with jax.named_scope("turn2"):
                lax.fori_loop(0, H, turn_ext, 0, unroll=H)
                lax.fori_loop(H + slots, near, turn_ext, 0, unroll=H)

        @pl.when(jnp.logical_and(step >= chunks, work < 0))
        def _():
            with jax.named_scope("build"):
                first = jnp.where(step == chunks, built, paused)
                lax.fori_loop(first, jnp.where(step == chunks, paused, slots), build, 0)

        @pl.when(work >= 0)
        def _():
            n = jnp.where(work == 0, 2 * parts, work - 1)

            @pl.when(n == 2 * parts - 1)
            def _():
                @pl.when(has_down)
                def _():
                    up.wait_recv()

                @pl.when(jnp.logical_not(has_down))
                def _():
                    for i in range(H):
                        edge[i] = zero

                @pl.when(has_up)
                def _():
                    down.wait_recv()

                @pl.when(jnp.logical_not(has_up))
                def _():
                    for i in range(H):
                        edge[H + i] = zero

            with jax.named_scope("gather"):
                gather_chunk(n)

        each(step, 1, event1)
        if piped:
            span_of(event2, ready(step - 1), ready(step))

        else:

            @pl.when(step == chunks + 2)
            def _():
                span_of(event2, 0, half)

        @pl.when(jnp.logical_and(work == jnp.where(z > 1, 1 - c, 0), has_down))
        def _():
            down.start()

        @pl.when(jnp.logical_and(work == 2 * c, has_up))
        def _():
            up.start()

        @pl.when(step == (steps - 4 + 2 * jnp.minimum(z, 1) + early if piped else steps - 1))
        def _():
            event3()

        return carry

    lax.fori_loop(0, steps, body, 0)

    with jax.named_scope("w3"):
        wait(r3.at[pl.ds(1, groups - 1)], q3)
    for j in range(groups):
        at = min(j * unit, padded - unit)
        length = min(unit, rows - at)
        wg_far[at : at + length, :] = r3[(g - j + groups) % groups, 0:length, :].astype(F32)

    with jax.named_scope("drain"):

        @pl.when(has_down)
        def _():
            halo_down.wait_send()
            down.wait_send()

        @pl.when(has_up)
        def _():
            halo_up.wait_send()
            up.wait_send()

        wait(r0, s0)
        wait(r1, s1)
        wait(r2.at[pl.ds(0, half - 1)], s2)
        wait(r3.at[pl.ds(1, groups - 1)], s3)


def finish_kernel(fin, wg_in, out_far, ig_far, wg_far, store):
    slots = out_far.shape[0]
    inner = slots - 2 * H
    moves = [
        (fin.at[pl.ds(0, slots)], out_far),
        (fin.at[pl.ds(slots, inner)], ig_far.at[pl.ds(H, inner)]),
        (fin.at[pl.ds(slots + inner, H)], ig_far.at[pl.ds(0, H)]),
        (fin.at[pl.ds(2 * slots - H, H)], ig_far.at[pl.ds(slots - H, H)]),
        (wg_in, wg_far),
    ]
    stores = [pltpu.make_async_copy(a, b, store.at[i]) for i, (a, b) in enumerate(moves)]
    for item in stores:
        item.start()
    for item in stores:
        item.wait()


def per_device(features, weights, cotangent, kernel_map, counts):
    voxels = features[0]
    slots, height, cin = voxels.shape
    offsets, _, cout = weights.shape
    space = lax.axis_size("space")
    groups = lax.axis_size("grp")
    near = slots + 2 * H

    half = space // 2
    deep = offsets * cin
    rows = deep // space
    padded = -(-rows // 16) * 16
    unit = -(-padded // (16 * groups)) * 16
    chunks = -(-offsets // SPAN)
    long = chunks * SPAN * cin
    direct = rows == padded
    piped = direct and half == chunks and 2 * rows <= SPAN * cin
    dma = pltpu.SemaphoreType.DMA
    vmem = pltpu.VMEM
    table = 2 * slots + near
    shapes = [((slots, height, cout), BF16), ((slots, height, cin), BF16), ((rows, cout), F32)]

    def stay(x):
        return pltpu.with_memory_space_constraint(x, pltpu.HBM)

    results = pl.pallas_call(
        functools.partial(main_kernel, groups, space, unit, rows, padded, piped),
        out_shape=(vmem((2 * slots + 2 * H, height, cout), BF16), vmem(*shapes[2])),
        in_specs=[FAR] * 5,
        out_specs=(VMEM, VMEM),
        scratch_shapes=[
            vmem((2 * offsets, cin, cout), BF16),
            vmem((slots, height, cout), BF16),
            vmem((slots, cout, height), BF16),
            vmem((slots * offsets + 1 + near, cin, height), BF16),
            vmem((near + 1, height, cin), BF16),
            vmem((H, height, cin), BF16),
            vmem((2 * H + 1, height, cin), BF16),
            vmem((table, 128), jnp.int32),
            pltpu.SMEM((table, 128), jnp.int32),
            pltpu.SMEM((1, 1), jnp.int32),
            vmem((slots, offsets), jnp.int32),
            vmem((16 if direct else long, cout), BF16),
            vmem((max(long, deep) if direct else space * padded, cout), BF16),
            vmem((half, padded, cout), BF16),
            vmem((half, padded, cout), BF16),
            vmem((half, groups - 1, unit, cout), BF16),
            vmem((half, unit, cout), BF16),
            vmem((half, unit, cout), BF16),
            vmem((groups, unit, cout), BF16),
            dma((7,)),
            dma((2,)), dma((2,)),
            dma((2,)), dma((2,)),
            dma, dma((half,)),
            dma, dma((half,)),
            dma, dma,
            dma, dma,
        ],
        compiler_params=pltpu.CompilerParams(
            collective_id=0, has_side_effects=True, vmem_limit_bytes=48 * 1024 * 1024
        ),
        name="main",
    )(counts, stay(kernel_map[0]), stay(voxels), stay(weights), stay(cotangent[0]))
    output, input_grad, wg = pl.pallas_call(
        finish_kernel,
        out_shape=tuple(jax.ShapeDtypeStruct(*x) for x in shapes),
        in_specs=[FAR] * 2,
        out_specs=(FAR,) * 3,
        scratch_shapes=[dma((5,))],
        compiler_params=pltpu.CompilerParams(vmem_limit_bytes=4 * 1024 * 1024),
        name="finish",
    )(*results)
    return output[None], input_grad[None], wg


def solution(mesh):
    in_specs = (
        P("grp", "space", None, None),
        P(),
        P("grp", "space", None, None),
        P("grp", "space", None),
        P("grp", "space"),
    )
    out_specs = (P("grp", "space", None, None), P("grp", "space", None, None), P("space", None))
    return jax.shard_map(
        per_device, mesh=mesh, in_specs=in_specs, out_specs=out_specs, check_vma=False
    )
```

```python
import functools

import jax
import jax.numpy as jnp
from jax import lax
from jax.experimental import pallas as pl
from jax.experimental.pallas import tpu as pltpu
from jax.sharding import PartitionSpec as P

H = 4
WIDE = 2 * H
SPAN = 7
BUILT, PAUSED = 11, 13
BF16, F32 = jnp.bfloat16, jnp.float32
VMEM = pl.BlockSpec(memory_space=pltpu.VMEM)
FAR = pl.BlockSpec(memory_space=pl.ANY)


def window_start(g, groups, unit, rows):
    return pl.multiple_of(g * unit - (g // (groups - 1)) * (groups * unit - rows), 16)


def main_kernel(
    groups, space, unit, rows, padded, piped,
    counts_far, map_far, feat, w_far, cot_far,
    fin, wg_far,
    w, cot, turned, blocks, ext, top, edge, tab, idx, counts, block_map,
    flat, part, r0, p1, r1, p2, r2, r3,
    sl, sh, qh, sr, qr, s0, q0, s1, q1, s2, q2, s3, q3,
):
    g = lax.axis_index("grp")
    s = lax.axis_index("space")
    half = space // 2
    z, c = s // 2, s % 2
    slots, height, cin = feat.shape
    offsets = block_map.shape[1]
    near = slots + 2 * H
    empty = slots * offsets
    base = empty + 1
    partner = (g, z * 2 + (1 - c))
    grp_peers = [((g + d) % groups, s) for d in range(1, groups)]
    z_peers = [(g, ((z + d) % half) * 2 + c) for d in range(1, half)]
    copy = pltpu.make_async_copy
    far = 3 - 2 * (g % 2)
    turns = [far, 4 - far, 2] if groups == 4 else list(range(1, groups))

    barrier = pltpu.get_barrier_semaphore()
    fixed = [partner] + grp_peers + z_peers
    for peer in fixed:
        pl.semaphore_signal(barrier, inc=1, device_id=peer, device_id_type=pl.DeviceIdType.MESH)
    across = s - 1 + 2 * c
    has_across = jnp.logical_and(across >= 0, across < space)

    @pl.when(has_across)
    def _():
        pl.semaphore_signal(barrier, inc=1, device_id=(g, across), device_id_type=pl.DeviceIdType.MESH)

    load_counts = copy(counts_far, counts, sl.at[5])
    load_map = copy(map_far, block_map, sl.at[6])
    load_counts.start()
    load_map.start()
    load_top = copy(feat.at[pl.ds(slots - H, H)], top, sl.at[4])
    load_cot = copy(cot_far, cot, sl.at[0])
    load_w = copy(w_far, w.at[pl.ds(offsets, offsets)], sl.at[1])
    load_feat = copy(feat, ext.at[pl.ds(1 + H, slots)], sl.at[2])
    load_top.start()
    load_cot.start()
    load_feat.start()
    load_w.start()

    zero = jnp.zeros((height, cin), BF16)
    blocks[empty] = zero
    ext[0] = zero
    edge[2 * H] = zero
    def remote(src, dst, send, recv, peer):
        return pltpu.make_async_remote_copy(
            src_ref=src, dst_ref=dst, send_sem=send, recv_sem=recv,
            device_id=peer, device_id_type=pl.DeviceIdType.MESH,
        )

    halo_down = remote(feat.at[pl.ds(0, H)], ext.at[pl.ds(1 + H + slots, H)], sh.at[0], qh.at[0], (g, s - 1))
    halo_up = remote(top, ext.at[pl.ds(1, H)], sh.at[1], qh.at[1], (g, s + 1))
    rim = 2 * slots
    down = remote(fin.at[pl.ds(rim, H)], edge.at[pl.ds(H, H)], sr.at[0], qr.at[0], (g, s - 1))
    up = remote(fin.at[pl.ds(rim + H, H)], edge.at[pl.ds(0, H)], sr.at[1], qr.at[1], (g, s + 1))
    has_down, has_up = s > 0, s < space - 1

    with jax.named_scope("barrier"):
        pl.semaphore_wait(barrier, len(fixed) + has_across.astype(jnp.int32))

    @pl.when(has_down)
    def _():
        halo_down.start()

    load_counts.wait()
    live = counts[0, 0]
    load_top.wait()
    for i in range(H):
        top[i] = top[i] * jnp.where(slots - H + i < live, 1.0, 0.0).astype(BF16)

    @pl.when(has_up)
    def _():
        halo_up.start()

    load_map.wait()

    row = lax.broadcasted_iota(jnp.int32, (slots, offsets), 0)
    lane = lax.broadcasted_iota(jnp.int32, (1, offsets), 1)
    source = block_map[...]
    local = source - (s * slots - H)
    dead = jnp.logical_and(local - H >= live, local < slots + H)
    skip = jnp.logical_or(jnp.logical_or(source < 0, row >= live), dead)
    place = jnp.where(skip, -1, local)
    tab[...] = jnp.full(tab.shape, empty, jnp.int32)
    tab[0:slots, 0:offsets] = place + base

    def pick(mask):
        found = jnp.max(jnp.where(mask, row, -1), axis=0, keepdims=True)
        return jnp.where(found < 0, empty, found * offsets + lane)

    def grad_row(a):
        if H <= a < 2 * H:
            return slots - 2 * H + a - H
        if slots <= a < slots + H:
            return slots - H + a - slots
        return slots + a if a < H else a - 2 * H if a < slots else a

    for a in range(near):
        at = slots + grad_row(a)
        tab[at : at + 1, 0:offsets] = pick(place == a)
    for b in range(slots):
        same = jnp.logical_and(place == place[b : b + 1, :], row < b)
        tab[slots + near + b : slots + near + b + 1, 0:offsets] = pick(same)
    load_idx = copy(tab, idx, sl.at[3])
    load_idx.start()

    load_cot.wait()

    def turn_cot(b, carry):
        turned[b] = cot[b].T
        return carry

    def turn_ext(i, carry):
        blocks[base + i] = ext[1 + i].T
        return carry

    def flip(k, carry):
        w[k] = w[offsets + k].T
        return carry

    def build(b, carry):
        mine = turned[b]

        def fetch(k):
            return mine + blocks[idx[slots + near + b, k]]

        ahead = fetch(0)
        for k in range(offsets):
            following = fetch(k + 1) if k + 1 < offsets else None
            blocks[b * offsets + k] = ahead
            ahead = following
        return carry

    with jax.named_scope("turncot"):
        lax.fori_loop(0, slots, turn_cot, 0, unroll=8)
    load_feat.wait()
    with jax.named_scope("turn"):
        lax.fori_loop(H, H + slots, turn_ext, 0, unroll=8)
    load_w.wait()
    with jax.named_scope("flip"):
        lax.fori_loop(0, offsets, flip, 0, unroll=9 if offsets % 9 == 0 else 1)
    load_idx.wait()
    built, paused = slots * BUILT // 16, slots * PAUSED // 16
    with jax.named_scope("build"):
        lax.fori_loop(0, built, build, 0)

    @pl.when(has_down)
    def _():
        with jax.named_scope("halo1"):
            halo_up.wait_recv()

    @pl.when(jnp.logical_not(has_down))
    def _():
        for i in range(H):
            ext[1 + i] = zero

    @pl.when(has_up)
    def _():
        with jax.named_scope("halo2"):
            halo_down.wait_recv()

    @pl.when(jnp.logical_not(has_up))
    def _():
        for i in range(H):
            ext[1 + H + slots + i] = zero

    parts = slots // WIDE
    chunks = -(-offsets // SPAN)
    direct = rows == padded

    def nth(t):
        return jnp.where(t == 0, 0, jnp.where(t == 1, half - 1, t - 1)) if piped else t

    def weight_chunk(t):
        spare = chunks * SPAN - offsets
        start = nth(t) * SPAN - (jnp.where(t == 1, spare, 0) if piped else 0)
        rhs = [
            jnp.concatenate([ext[idx[b, start + k] - empty] for b in range(slots)], axis=0)
            for k in range(SPAN)
        ]
        lhs = jnp.concatenate([turned[b] for b in range(slots)], axis=1)
        got = jnp.dot(lhs, jnp.concatenate(rhs, axis=1), preferred_element_type=F32)
        into = part if direct else flat
        for k in range(SPAN):
            to = start + k
            if piped and k >= SPAN - spare:
                to = jnp.where(t == chunks - 1, (chunks - 1) * SPAN + k, to)
            at = pl.multiple_of(to * cin, cin)
            into[pl.ds(at, cin), :] = got[:, k * cin : (k + 1) * cin].astype(BF16).T

    def gather_chunk(n):
        kind = jnp.where(n >= parts, offsets, 0)
        lhs = jnp.concatenate([w[kind + k] for k in range(offsets)], axis=1)
        rhs = [
            jnp.concatenate([blocks[idx[n * WIDE + j, k]] for j in range(WIDE)], axis=1)
            for k in range(offsets)
        ]
        got = jnp.dot(lhs, jnp.concatenate(rhs, axis=0), preferred_element_type=F32)
        outer = n == 2 * parts - 1
        for j in range(WIDE):
            i = jnp.where(n < parts, n, n - parts) * WIDE + j
            i = jnp.where(n < parts, i, jnp.where(outer, j if j < H else slots - WIDE + j, i + H))
            extra = jnp.where(outer, j, 2 * H)
            factor = jnp.where(jnp.logical_or(n == 2 * parts, i < live), 1.0, 0.0).astype(F32)
            value = got[:, j * height : (j + 1) * height].T + edge[extra].astype(F32)
            fin[n * WIDE + j] = (value * factor).astype(BF16)

    def piece(p):
        return pl.ds(pl.multiple_of(p * padded, 16), padded)

    here = window_start(g, groups, unit, padded)

    def copy0(i):
        return remote(part.at[piece(2 * i + 1 - c)], r0.at[i], s0, q0.at[i], partner)

    def copy1(i, d):
        there = window_start((g + d) % groups, groups, unit, padded)
        return remote(
            p1.at[i, pl.ds(there, unit)], r1.at[i, d - 1], s1, q1.at[i], ((g + d) % groups, s)
        )

    def copy2(i, slot):
        return remote(p2.at[i], r2.at[slot], s2, q2, (g, 2 * i + c))

    def wait(like, sem):
        copy(like, like, sem).wait()

    def copy3(d):
        return remote(r3.at[0], r3.at[d], s3, q3, ((g + d) % groups, s))

    def event0(t):
        i = nth(t)
        copy0(i).start()

    def event1(t):
        i = nth(t)
        with jax.named_scope("w0"):
            copy0(i).wait_recv()
        p1[i] = (part[piece(2 * i + c), :].astype(F32) + r0[i].astype(F32)).astype(BF16)
        for d in turns:
            copy1(i, d).start()

    def event2(t):
        i = nth(t)
        total = p1[i, pl.ds(here, unit), :].astype(F32)
        with jax.named_scope("w1"):
            wait(r1.at[i], q1.at[i])
        for d in range(1, groups):
            total = total + r1[i, d - 1].astype(F32)
        p2[i] = total.astype(BF16)

        @pl.when(z != i)
        def _():
            copy2(i, z).start()

    def event3():
        with jax.named_scope("w2"):
            wait(r2.at[pl.ds(0, half - 1)], q2)
        r2[z] = p2[z]
        total = jnp.zeros((unit, cot.shape[2]), F32)
        for i in range(half):
            total = total + r2[i].astype(F32)
        r3[0] = total.astype(BF16)
        for d in turns:
            copy3(d).start()

    def span_of(event, first, past):
        lax.fori_loop(first, past, lambda i, carry: (event(i), carry)[1], 0)

    def each(step, lag, event):
        if piped:
            i = step - lag

            @pl.when(jnp.logical_and(i >= 0, i < half))
            def _():
                event(i)

        else:

            @pl.when(step == chunks - 1 + lag)
            def _():
                span_of(event, 0, half)

    steps = chunks + 3 + 2 * parts

    early = jnp.where(jnp.logical_and(z == 0, g == 0), 1, 0)

    def ready(step):
        counts_at = [jnp.minimum(z, 1), 2, half - early]
        number = jnp.where(step > chunks, half, 0)
        for j, value in enumerate(counts_at):
            number = jnp.where(step == chunks + 1 + j, value, number)
        return number

    def body(step, carry):
        work = step - chunks - 2

        @pl.when(step < chunks)
        def _():
            with jax.named_scope("wg"):
                weight_chunk(step)

        if not direct:

            @pl.when(step == chunks - 1)
            def _():
                for p in range(space):
                    part[p * padded : p * padded + rows, :] = flat[p * rows : (p + 1) * rows, :]
                    part[p * padded + rows : (p + 1) * padded, :] = jnp.zeros((padded - rows, part.shape[1]), BF16)

        each(step, 0, event0)

        @pl.when(step == chunks)
        def _():
            with jax.named_scope("turn2"):
                lax.fori_loop(0, H, turn_ext, 0, unroll=H)
                lax.fori_loop(H + slots, near, turn_ext, 0, unroll=H)

        @pl.when(jnp.logical_and(step >= chunks, work < 0))
        def _():
            with jax.named_scope("build"):
                first = jnp.where(step == chunks, built, paused)
                lax.fori_loop(first, jnp.where(step == chunks, paused, slots), build, 0)

        @pl.when(work >= 0)
        def _():
            n = jnp.where(work == 0, 2 * parts, work - 1)

            @pl.when(n == 2 * parts - 1)
            def _():
                @pl.when(has_down)
                def _():
                    up.wait_recv()

                @pl.when(jnp.logical_not(has_down))
                def _():
                    for i in range(H):
                        edge[i] = zero

                @pl.when(has_up)
                def _():
                    down.wait_recv()

                @pl.when(jnp.logical_not(has_up))
                def _():
                    for i in range(H):
                        edge[H + i] = zero

            with jax.named_scope("gather"):
                gather_chunk(n)

        each(step, 1, event1)
        if piped:
            span_of(event2, ready(step - 1), ready(step))

        else:

            @pl.when(step == chunks + 2)
            def _():
                span_of(event2, 0, half)

        @pl.when(jnp.logical_and(work == jnp.where(z > 1, 1 - c, 0), has_down))
        def _():
            down.start()

        @pl.when(jnp.logical_and(work == 2 * c, has_up))
        def _():
            up.start()

        @pl.when(step == (steps - 4 + 2 * jnp.minimum(z, 1) + early if piped else steps - 1))
        def _():
            event3()

        return carry

    lax.fori_loop(0, steps, body, 0)

    with jax.named_scope("w3"):
        wait(r3.at[pl.ds(1, groups - 1)], q3)
    for j in range(groups):
        at = min(j * unit, padded - unit)
        length = min(unit, rows - at)
        wg_far[at : at + length, :] = r3[(g - j + groups) % groups, 0:length, :].astype(F32)

    with jax.named_scope("drain"):

        @pl.when(has_down)
        def _():
            halo_down.wait_send()
            down.wait_send()

        @pl.when(has_up)
        def _():
            halo_up.wait_send()
            up.wait_send()

        wait(r0, s0)
        wait(r1, s1)
        wait(r2.at[pl.ds(0, half - 1)], s2)
        wait(r3.at[pl.ds(1, groups - 1)], s3)


def finish_kernel(fin, wg_in, out_far, ig_far, wg_far, store):
    slots = out_far.shape[0]
    inner = slots - 2 * H
    moves = [
        (fin.at[pl.ds(0, slots)], out_far),
        (fin.at[pl.ds(slots, inner)], ig_far.at[pl.ds(H, inner)]),
        (fin.at[pl.ds(slots + inner, H)], ig_far.at[pl.ds(0, H)]),
        (fin.at[pl.ds(2 * slots - H, H)], ig_far.at[pl.ds(slots - H, H)]),
        (wg_in, wg_far),
    ]
    stores = [pltpu.make_async_copy(a, b, store.at[i]) for i, (a, b) in enumerate(moves)]
    for item in stores:
        item.start()
    for item in stores:
        item.wait()


def per_device(features, weights, cotangent, kernel_map, counts):
    voxels = features[0]
    slots, height, cin = voxels.shape
    offsets, _, cout = weights.shape
    space = lax.axis_size("space")
    groups = lax.axis_size("grp")
    near = slots + 2 * H

    half = space // 2
    deep = offsets * cin
    rows = deep // space
    padded = -(-rows // 16) * 16
    unit = -(-padded // (16 * groups)) * 16
    chunks = -(-offsets // SPAN)
    long = chunks * SPAN * cin
    direct = rows == padded
    piped = direct and half == chunks and 2 * rows <= SPAN * cin
    dma = pltpu.SemaphoreType.DMA
    vmem = pltpu.VMEM
    table = 2 * slots + near
    shapes = [((slots, height, cout), BF16), ((slots, height, cin), BF16), ((rows, cout), F32)]

    def stay(x):
        return pltpu.with_memory_space_constraint(x, pltpu.HBM)

    results = pl.pallas_call(
        functools.partial(main_kernel, groups, space, unit, rows, padded, piped),
        out_shape=(vmem((2 * slots + 2 * H, height, cout), BF16), vmem(*shapes[2])),
        in_specs=[FAR] * 5,
        out_specs=(VMEM, VMEM),
        scratch_shapes=[
            vmem((2 * offsets, cin, cout), BF16),
            vmem((slots, height, cout), BF16),
            vmem((slots, cout, height), BF16),
            vmem((slots * offsets + 1 + near, cin, height), BF16),
            vmem((near + 1, height, cin), BF16),
            vmem((H, height, cin), BF16),
            vmem((2 * H + 1, height, cin), BF16),
            vmem((table, 128), jnp.int32),
            pltpu.SMEM((table, 128), jnp.int32),
            pltpu.SMEM((1, 1), jnp.int32),
            vmem((slots, offsets), jnp.int32),
            vmem((16 if direct else long, cout), BF16),
            vmem((max(long, deep) if direct else space * padded, cout), BF16),
            vmem((half, padded, cout), BF16),
            vmem((half, padded, cout), BF16),
            vmem((half, groups - 1, unit, cout), BF16),
            vmem((half, unit, cout), BF16),
            vmem((half, unit, cout), BF16),
            vmem((groups, unit, cout), BF16),
            dma((7,)),
            dma((2,)), dma((2,)),
            dma((2,)), dma((2,)),
            dma, dma((half,)),
            dma, dma((half,)),
            dma, dma,
            dma, dma,
        ],
        compiler_params=pltpu.CompilerParams(
            collective_id=0, has_side_effects=True, vmem_limit_bytes=48 * 1024 * 1024
        ),
        name="main",
    )(counts, stay(kernel_map[0]), stay(voxels), stay(weights), stay(cotangent[0]))
    output, input_grad, wg = pl.pallas_call(
        finish_kernel,
        out_shape=tuple(jax.ShapeDtypeStruct(*x) for x in shapes),
        in_specs=[FAR] * 2,
        out_specs=(FAR,) * 3,
        scratch_shapes=[dma((5,))],
        compiler_params=pltpu.CompilerParams(vmem_limit_bytes=4 * 1024 * 1024),
        name="finish",
    )(*results)
    return output[None], input_grad[None], wg


def solution(mesh):
    in_specs = (
        P("grp", "space", None, None),
        P(),
        P("grp", "space", None, None),
        P("grp", "space", None),
        P("grp", "space"),
    )
    out_specs = (P("grp", "space", None, None), P("grp", "space", None, None), P("space", None))
    return jax.shard_map(
        per_device, mesh=mesh, in_specs=in_specs, out_specs=out_specs, check_vma=False
    )
```

```python
import functools

import jax
import jax.numpy as jnp
from jax import lax
from jax.experimental import pallas as pl
from jax.experimental.pallas import tpu as pltpu
from jax.sharding import PartitionSpec as P

H = 4
WIDE = 2 * H
SPAN = 7
BUILT, PAUSED = 12, 14
BF16, F32 = jnp.bfloat16, jnp.float32
VMEM = pl.BlockSpec(memory_space=pltpu.VMEM)
FAR = pl.BlockSpec(memory_space=pl.ANY)


def window_start(g, groups, unit, rows):
    return pl.multiple_of(g * unit - (g // (groups - 1)) * (groups * unit - rows), 16)


def main_kernel(
    groups, space, unit, rows, padded, piped,
    counts_far, map_far, feat, w_far, cot_far,
    fin, wg_far,
    w, cot, turned, blocks, ext, top, edge, tab, idx, counts, block_map,
    flat, part, r0, p1, r1, p2, r2, r3,
    sl, sh, qh, sr, qr, s0, q0, s1, q1, s2, q2, s3, q3,
):
    g = lax.axis_index("grp")
    s = lax.axis_index("space")
    half = space // 2
    z, c = s // 2, s % 2
    slots, height, cin = feat.shape
    offsets = block_map.shape[1]
    near = slots + 2 * H
    empty = slots * offsets
    base = empty + 1
    partner = (g, z * 2 + (1 - c))
    grp_peers = [((g + d) % groups, s) for d in range(1, groups)]
    z_peers = [(g, ((z + d) % half) * 2 + c) for d in range(1, half)]
    copy = pltpu.make_async_copy
    far = 3 - 2 * (g % 2)
    turns = [far, 2, 4 - far] if groups == 4 else list(range(1, groups))

    barrier = pltpu.get_barrier_semaphore()
    fixed = [partner] + grp_peers + z_peers
    for peer in fixed:
        pl.semaphore_signal(barrier, inc=1, device_id=peer, device_id_type=pl.DeviceIdType.MESH)
    across = s - 1 + 2 * c
    has_across = jnp.logical_and(across >= 0, across < space)

    @pl.when(has_across)
    def _():
        pl.semaphore_signal(barrier, inc=1, device_id=(g, across), device_id_type=pl.DeviceIdType.MESH)

    load_counts = copy(counts_far, counts, sl.at[5])
    load_map = copy(map_far, block_map, sl.at[6])
    load_counts.start()
    load_map.start()
    load_top = copy(feat.at[pl.ds(slots - H, H)], top, sl.at[4])
    load_cot = copy(cot_far, cot, sl.at[0])
    load_w = copy(w_far, w.at[pl.ds(offsets, offsets)], sl.at[1])
    load_feat = copy(feat, ext.at[pl.ds(1 + H, slots)], sl.at[2])
    load_top.start()
    load_cot.start()
    load_feat.start()
    load_w.start()

    zero = jnp.zeros((height, cin), BF16)
    blocks[empty] = zero
    ext[0] = zero
    edge[2 * H] = zero
    def remote(src, dst, send, recv, peer):
        return pltpu.make_async_remote_copy(
            src_ref=src, dst_ref=dst, send_sem=send, recv_sem=recv,
            device_id=peer, device_id_type=pl.DeviceIdType.MESH,
        )

    halo_down = remote(feat.at[pl.ds(0, H)], ext.at[pl.ds(1 + H + slots, H)], sh.at[0], qh.at[0], (g, s - 1))
    halo_up = remote(top, ext.at[pl.ds(1, H)], sh.at[1], qh.at[1], (g, s + 1))
    rim = 2 * slots
    down = remote(fin.at[pl.ds(rim, H)], edge.at[pl.ds(H, H)], sr.at[0], qr.at[0], (g, s - 1))
    up = remote(fin.at[pl.ds(rim + H, H)], edge.at[pl.ds(0, H)], sr.at[1], qr.at[1], (g, s + 1))
    has_down, has_up = s > 0, s < space - 1

    with jax.named_scope("barrier"):
        pl.semaphore_wait(barrier, len(fixed) + has_across.astype(jnp.int32))

    @pl.when(has_down)
    def _():
        halo_down.start()

    load_counts.wait()
    live = counts[0, 0]
    load_top.wait()
    for i in range(H):
        top[i] = top[i] * jnp.where(slots - H + i < live, 1.0, 0.0).astype(BF16)

    @pl.when(has_up)
    def _():
        halo_up.start()

    load_map.wait()

    row = lax.broadcasted_iota(jnp.int32, (slots, offsets), 0)
    lane = lax.broadcasted_iota(jnp.int32, (1, offsets), 1)
    source = block_map[...]
    local = source - (s * slots - H)
    dead = jnp.logical_and(local - H >= live, local < slots + H)
    skip = jnp.logical_or(jnp.logical_or(source < 0, row >= live), dead)
    place = jnp.where(skip, -1, local)
    tab[...] = jnp.full(tab.shape, empty, jnp.int32)
    tab[0:slots, 0:offsets] = place + base

    def pick(mask):
        found = jnp.max(jnp.where(mask, row, -1), axis=0, keepdims=True)
        return jnp.where(found < 0, empty, found * offsets + lane)

    def grad_row(a):
        if H <= a < 2 * H:
            return slots - 2 * H + a - H
        if slots <= a < slots + H:
            return slots - H + a - slots
        return slots + a if a < H else a - 2 * H if a < slots else a

    for a in range(near):
        at = slots + grad_row(a)
        tab[at : at + 1, 0:offsets] = pick(place == a)
    for b in range(slots):
        same = jnp.logical_and(place == place[b : b + 1, :], row < b)
        tab[slots + near + b : slots + near + b + 1, 0:offsets] = pick(same)
    load_idx = copy(tab, idx, sl.at[3])
    load_idx.start()

    load_cot.wait()

    def turn_cot(b, carry):
        turned[b] = cot[b].T
        return carry

    def turn_ext(i, carry):
        blocks[base + i] = ext[1 + i].T
        return carry

    def flip(k, carry):
        w[k] = w[offsets + k].T
        return carry

    def build(b, carry):
        mine = turned[b]

        def fetch(k):
            return mine + blocks[idx[slots + near + b, k]]

        ahead = fetch(0)
        for k in range(offsets):
            following = fetch(k + 1) if k + 1 < offsets else None
            blocks[b * offsets + k] = ahead
            ahead = following
        return carry

    with jax.named_scope("turncot"):
        lax.fori_loop(0, slots, turn_cot, 0, unroll=8)
    load_feat.wait()
    with jax.named_scope("turn"):
        lax.fori_loop(H, H + slots, turn_ext, 0, unroll=8)
    load_w.wait()
    with jax.named_scope("flip"):
        lax.fori_loop(0, offsets, flip, 0, unroll=9 if offsets % 9 == 0 else 1)
    load_idx.wait()
    built, paused = slots * BUILT // 16, slots * PAUSED // 16
    with jax.named_scope("build"):
        lax.fori_loop(0, built, build, 0)

    @pl.when(has_down)
    def _():
        with jax.named_scope("halo1"):
            halo_up.wait_recv()

    @pl.when(jnp.logical_not(has_down))
    def _():
        for i in range(H):
            ext[1 + i] = zero

    @pl.when(has_up)
    def _():
        with jax.named_scope("halo2"):
            halo_down.wait_recv()

    @pl.when(jnp.logical_not(has_up))
    def _():
        for i in range(H):
            ext[1 + H + slots + i] = zero

    parts = slots // WIDE
    chunks = -(-offsets // SPAN)
    direct = rows == padded

    def nth(t):
        return jnp.where(t == 0, 0, jnp.where(t == 1, half - 1, t - 1)) if piped else t

    def weight_chunk(t):
        spare = chunks * SPAN - offsets
        start = nth(t) * SPAN - (jnp.where(t == 1, spare, 0) if piped else 0)
        rhs = [
            jnp.concatenate([ext[idx[b, start + k] - empty] for b in range(slots)], axis=0)
            for k in range(SPAN)
        ]
        lhs = jnp.concatenate([turned[b] for b in range(slots)], axis=1)
        got = jnp.dot(lhs, jnp.concatenate(rhs, axis=1), preferred_element_type=F32)
        into = part if direct else flat
        for k in range(SPAN):
            to = start + k
            if piped and k >= SPAN - spare:
                to = jnp.where(t == chunks - 1, (chunks - 1) * SPAN + k, to)
            at = pl.multiple_of(to * cin, cin)
            into[pl.ds(at, cin), :] = got[:, k * cin : (k + 1) * cin].astype(BF16).T

    def gather_chunk(n):
        kind = jnp.where(n >= parts, offsets, 0)
        lhs = jnp.concatenate([w[kind + k] for k in range(offsets)], axis=1)
        rhs = [
            jnp.concatenate([blocks[idx[n * WIDE + j, k]] for j in range(WIDE)], axis=1)
            for k in range(offsets)
        ]
        got = jnp.dot(lhs, jnp.concatenate(rhs, axis=0), preferred_element_type=F32)
        outer = n == 2 * parts - 1
        for j in range(WIDE):
            i = jnp.where(n < parts, n, n - parts) * WIDE + j
            i = jnp.where(n < parts, i, jnp.where(outer, j if j < H else slots - WIDE + j, i + H))
            extra = jnp.where(outer, j, 2 * H)
            factor = jnp.where(jnp.logical_or(n == 2 * parts, i < live), 1.0, 0.0).astype(F32)
            value = got[:, j * height : (j + 1) * height].T + edge[extra].astype(F32)
            fin[n * WIDE + j] = (value * factor).astype(BF16)

    def piece(p):
        return pl.ds(pl.multiple_of(p * padded, 16), padded)

    here = window_start(g, groups, unit, padded)

    def copy0(i):
        return remote(part.at[piece(2 * i + 1 - c)], r0.at[i], s0, q0.at[i], partner)

    def copy1(i, d):
        there = window_start((g + d) % groups, groups, unit, padded)
        return remote(
            p1.at[i, pl.ds(there, unit)], r1.at[i, d - 1], s1, q1.at[i], ((g + d) % groups, s)
        )

    def copy2(i, slot):
        return remote(p2.at[i], r2.at[slot], s2, q2, (g, 2 * i + c))

    def wait(like, sem):
        copy(like, like, sem).wait()

    def copy3(d):
        return remote(r3.at[0], r3.at[d], s3, q3, ((g + d) % groups, s))

    def event0(t):
        i = nth(t)
        copy0(i).start()

    def event1(t):
        i = nth(t)
        with jax.named_scope("w0"):
            copy0(i).wait_recv()
        p1[i] = (part[piece(2 * i + c), :].astype(F32) + r0[i].astype(F32)).astype(BF16)
        for d in turns:
            copy1(i, d).start()

    def event2(t):
        i = nth(t)
        total = p1[i, pl.ds(here, unit), :].astype(F32)
        with jax.named_scope("w1"):
            wait(r1.at[i], q1.at[i])
        for d in range(1, groups):
            total = total + r1[i, d - 1].astype(F32)
        p2[i] = total.astype(BF16)

        @pl.when(z != i)
        def _():
            copy2(i, z).start()

    def event3():
        with jax.named_scope("w2"):
            wait(r2.at[pl.ds(0, half - 1)], q2)
        r2[z] = p2[z]
        total = jnp.zeros((unit, cot.shape[2]), F32)
        for i in range(half):
            total = total + r2[i].astype(F32)
        r3[0] = total.astype(BF16)
        for d in turns:
            copy3(d).start()

    def span_of(event, first, past):
        lax.fori_loop(first, past, lambda i, carry: (event(i), carry)[1], 0)

    def each(step, lag, event):
        if piped:
            i = step - lag

            @pl.when(jnp.logical_and(i >= 0, i < half))
            def _():
                event(i)

        else:

            @pl.when(step == chunks - 1 + lag)
            def _():
                span_of(event, 0, half)

    steps = chunks + 3 + 2 * parts

    early = jnp.where(jnp.logical_and(z == 0, g == 0), 1, 0)

    def ready(step):
        counts_at = [jnp.minimum(z, 1), 2, half - early]
        number = jnp.where(step > chunks, half, 0)
        for j, value in enumerate(counts_at):
            number = jnp.where(step == chunks + 1 + j, value, number)
        return number

    def body(step, carry):
        work = step - chunks - 2

        @pl.when(step < chunks)
        def _():
            with jax.named_scope("wg"):
                weight_chunk(step)

        if not direct:

            @pl.when(step == chunks - 1)
            def _():
                for p in range(space):
                    part[p * padded : p * padded + rows, :] = flat[p * rows : (p + 1) * rows, :]
                    part[p * padded + rows : (p + 1) * padded, :] = jnp.zeros((padded - rows, part.shape[1]), BF16)

        each(step, 0, event0)

        @pl.when(step == chunks)
        def _():
            with jax.named_scope("turn2"):
                lax.fori_loop(0, H, turn_ext, 0, unroll=H)
                lax.fori_loop(H + slots, near, turn_ext, 0, unroll=H)

        @pl.when(jnp.logical_and(step >= chunks, work < 0))
        def _():
            with jax.named_scope("build"):
                first = jnp.where(step == chunks, built, paused)
                lax.fori_loop(first, jnp.where(step == chunks, paused, slots), build, 0)

        @pl.when(work >= 0)
        def _():
            n = jnp.where(work == 0, 2 * parts, work - 1)

            @pl.when(n == 2 * parts - 1)
            def _():
                @pl.when(has_down)
                def _():
                    up.wait_recv()

                @pl.when(jnp.logical_not(has_down))
                def _():
                    for i in range(H):
                        edge[i] = zero

                @pl.when(has_up)
                def _():
                    down.wait_recv()

                @pl.when(jnp.logical_not(has_up))
                def _():
                    for i in range(H):
                        edge[H + i] = zero

            with jax.named_scope("gather"):
                gather_chunk(n)

        each(step, 1, event1)
        if piped:
            span_of(event2, ready(step - 1), ready(step))

        else:

            @pl.when(step == chunks + 2)
            def _():
                span_of(event2, 0, half)

        @pl.when(jnp.logical_and(work == jnp.where(z > 1, 1 - c, 0), has_down))
        def _():
            down.start()

        @pl.when(jnp.logical_and(work == 2 * c, has_up))
        def _():
            up.start()

        @pl.when(step == (steps - 4 + 2 * jnp.minimum(z, 1) + early if piped else steps - 1))
        def _():
            event3()

        return carry

    lax.fori_loop(0, steps, body, 0)

    with jax.named_scope("w3"):
        wait(r3.at[pl.ds(1, groups - 1)], q3)
    for j in range(groups):
        at = min(j * unit, padded - unit)
        length = min(unit, rows - at)
        wg_far[at : at + length, :] = r3[(g - j + groups) % groups, 0:length, :].astype(F32)

    with jax.named_scope("drain"):

        @pl.when(has_down)
        def _():
            halo_down.wait_send()
            down.wait_send()

        @pl.when(has_up)
        def _():
            halo_up.wait_send()
            up.wait_send()

        wait(r0, s0)
        wait(r1, s1)
        wait(r2.at[pl.ds(0, half - 1)], s2)
        wait(r3.at[pl.ds(1, groups - 1)], s3)


def finish_kernel(fin, wg_in, out_far, ig_far, wg_far, store):
    slots = out_far.shape[0]
    inner = slots - 2 * H
    moves = [
        (fin.at[pl.ds(0, slots)], out_far),
        (fin.at[pl.ds(slots, inner)], ig_far.at[pl.ds(H, inner)]),
        (fin.at[pl.ds(slots + inner, H)], ig_far.at[pl.ds(0, H)]),
        (fin.at[pl.ds(2 * slots - H, H)], ig_far.at[pl.ds(slots - H, H)]),
        (wg_in, wg_far),
    ]
    stores = [pltpu.make_async_copy(a, b, store.at[i]) for i, (a, b) in enumerate(moves)]
    for item in stores:
        item.start()
    for item in stores:
        item.wait()


def per_device(features, weights, cotangent, kernel_map, counts):
    voxels = features[0]
    slots, height, cin = voxels.shape
    offsets, _, cout = weights.shape
    space = lax.axis_size("space")
    groups = lax.axis_size("grp")
    near = slots + 2 * H

    half = space // 2
    deep = offsets * cin
    rows = deep // space
    padded = -(-rows // 16) * 16
    unit = -(-padded // (16 * groups)) * 16
    chunks = -(-offsets // SPAN)
    long = chunks * SPAN * cin
    direct = rows == padded
    piped = direct and half == chunks and 2 * rows <= SPAN * cin
    dma = pltpu.SemaphoreType.DMA
    vmem = pltpu.VMEM
    table = 2 * slots + near
    shapes = [((slots, height, cout), BF16), ((slots, height, cin), BF16), ((rows, cout), F32)]

    def stay(x):
        return pltpu.with_memory_space_constraint(x, pltpu.HBM)

    results = pl.pallas_call(
        functools.partial(main_kernel, groups, space, unit, rows, padded, piped),
        out_shape=(vmem((2 * slots + 2 * H, height, cout), BF16), vmem(*shapes[2])),
        in_specs=[FAR] * 5,
        out_specs=(VMEM, VMEM),
        scratch_shapes=[
            vmem((2 * offsets, cin, cout), BF16),
            vmem((slots, height, cout), BF16),
            vmem((slots, cout, height), BF16),
            vmem((slots * offsets + 1 + near, cin, height), BF16),
            vmem((near + 1, height, cin), BF16),
            vmem((H, height, cin), BF16),
            vmem((2 * H + 1, height, cin), BF16),
            vmem((table, 128), jnp.int32),
            pltpu.SMEM((table, 128), jnp.int32),
            pltpu.SMEM((1, 1), jnp.int32),
            vmem((slots, offsets), jnp.int32),
            vmem((16 if direct else long, cout), BF16),
            vmem((max(long, deep) if direct else space * padded, cout), BF16),
            vmem((half, padded, cout), BF16),
            vmem((half, padded, cout), BF16),
            vmem((half, groups - 1, unit, cout), BF16),
            vmem((half, unit, cout), BF16),
            vmem((half, unit, cout), BF16),
            vmem((groups, unit, cout), BF16),
            dma((7,)),
            dma((2,)), dma((2,)),
            dma((2,)), dma((2,)),
            dma, dma((half,)),
            dma, dma((half,)),
            dma, dma,
            dma, dma,
        ],
        compiler_params=pltpu.CompilerParams(
            collective_id=0, has_side_effects=True, vmem_limit_bytes=48 * 1024 * 1024
        ),
        name="main",
    )(counts, stay(kernel_map[0]), stay(voxels), stay(weights), stay(cotangent[0]))
    output, input_grad, wg = pl.pallas_call(
        finish_kernel,
        out_shape=tuple(jax.ShapeDtypeStruct(*x) for x in shapes),
        in_specs=[FAR] * 2,
        out_specs=(FAR,) * 3,
        scratch_shapes=[dma((5,))],
        compiler_params=pltpu.CompilerParams(vmem_limit_bytes=4 * 1024 * 1024),
        name="finish",
    )(*results)
    return output[None], input_grad[None], wg


def solution(mesh):
    in_specs = (
        P("grp", "space", None, None),
        P(),
        P("grp", "space", None, None),
        P("grp", "space", None),
        P("grp", "space"),
    )
    out_specs = (P("grp", "space", None, None), P("grp", "space", None, None), P("space", None))
    return jax.shard_map(
        per_device, mesh=mesh, in_specs=in_specs, out_specs=out_specs, check_vma=False
    )
```
